32 devices in a mesh: groups: 2 (over x), expert: 16 (over z, y, core).
Axes of the slice: x: 2, y: 2, z: 4, core: 2. Of those that a mesh axis runs over, the one named last changes fastest.
Arguments:
- tokens: bfloat16 [2048, 2048], P(('groups', 'expert')), parts along dimension 0, may hold values from -6 to 6
- grad_out: bfloat16 [2048, 2048], P(('groups', 'expert')), parts along dimension 0, may hold values from -3 to 3
- expert_ids: int32 [2048, 4], P(('groups', 'expert')), parts along dimension 0, may hold values from 0 to 7, as said below
- router_weight: bfloat16 [2048, 8], replicated, may hold values from -0.125 to 0.125
- gate_weight: bfloat16 [16, 2048, 384], P('expert'), may hold values from -0.125 to 0.125
- up_weight: bfloat16 [16, 2048, 384], P('expert'), may hold values from -0.125 to 0.125
- down_weight: bfloat16 [16, 384, 2048], P('expert'), may hold values from -0.21875 to 0.21875
Outputs:
- mixed: bfloat16 [2048, 2048], P(('groups', 'expert')), parts along dimension 0
- token_grad: bfloat16 [2048, 2048], P(('groups', 'expert')), parts along dimension 0
- gate_grad: bfloat16 [32, 2048, 384], P(('groups', 'expert')), parts along dimension 0
- up_grad: bfloat16 [32, 2048, 384], P(('groups', 'expert')), parts along dimension 0
- down_grad: bfloat16 [32, 384, 2048], P(('groups', 'expert')), parts along dimension 0
- router_grad: float32 [4096, 8], P(('groups', 'expert')), parts along dimension 0
The draws below stay inside these ranges and needn't reach their ends.
There are 2 independent parts, one for each index of `groups`. The reference program is written for one: setup_inputs(seed, part) draws one part's arguments, and reference() takes and returns one part's arrays. A program takes and returns all parts, laid end to end along the dimension named above; an argument that names none is the same for every part. Nothing has to cross between parts.
Inputs may be any that keep to these rules, and one draw needn't show every extreme that they name: `expert_ids`: each token names 4 different experts. In each aligned block of 32 tokens (either half of one device's tokens) no expert is named by more than 32 tokens, and some expert by exactly 32 in every block.
All inputs are finite; a program needn't handle non-finite values.
Results may differ from the reference program's by a relative error of at most 0.009.
Values may be sent and summed in bfloat16 or wider, within the bound.
No kernel may reach another device: no remote copies, remote signals or barrier semaphores. Data moves between devices by JAX's collectives and lax.ppermute only.
A program may use at most 128 MiB of HBM per device.

```python
import jax
import jax.numpy as jnp
from jax import lax

D = 2048
FF = 768
TOP = 4
TOK_DEV = 64
EXPERTS = 8
TOKENS = 1024
CAP_PEER = 32
N_EXPERT = 16


def draw_expert_ids(key, part):
    halfway = TOK_DEV // 2
    blocks = TOKENS // halfway
    hotter = max(EXPERTS // 8, 1)
    leftover = halfway * TOP - hotter * CAP_PEER
    colder = EXPERTS - hotter
    base_count = leftover // colder
    extra_count = leftover % colder
    cold_counts = jnp.where(jnp.arange(colder) < extra_count, base_count + 1, base_count).astype(jnp.int32)
    ranking = jax.random.permutation(jax.random.fold_in(key, 11), EXPERTS)
    block_keys = jax.random.split(jax.random.fold_in(key, 23), blocks)

    def one_block(block_key):
        first_key, second_key = jax.random.split(block_key)
        shuffled = cold_counts[jax.random.permutation(first_key, colder)]
        per_rank = jnp.concatenate([jnp.full((hotter,), CAP_PEER, jnp.int32), shuffled])
        counts = jnp.zeros((EXPERTS,), jnp.int32).at[ranking].set(per_rank)
        ends = jnp.cumsum(counts)
        position = jnp.arange(halfway * TOP, dtype=jnp.int32)
        listed = jnp.sum((position[:, None] >= ends[None, :]).astype(jnp.int32), axis=1)
        table = listed.reshape(TOP, halfway).T
        shuffle = jax.random.permutation(second_key, halfway)
        return table[shuffle]
    chosen = jax.vmap(one_block)(block_keys)
    return chosen.reshape(TOKENS, TOP).astype(jnp.int32)


def spiked(result, rng, source, target, shards_of, factor):
    owner, partner = [(jnp.arange(result.shape[dim]) // (result.shape[dim] // shards_of)).reshape([-1 if axis == dim else 1 for axis in range(result.ndim)]) for dim in (source, target)]
    chosen = jax.random.permutation(rng, shards_of)[partner]
    strong = (owner == chosen) | (owner == (partner + shards_of // 2) % shards_of)
    return jnp.where(strong, factor * result, result)


def shard_levels(key, extent, cuts, smallest, high):
    def one(dim, blocks):
        draws = jax.random.uniform(jax.random.fold_in(jax.random.fold_in(key, 6), dim), (blocks,), jnp.float32, smallest / len(cuts), high / len(cuts))
        return jnp.repeat(jnp.exp(draws), extent[dim] // blocks).reshape((-1,) + (1,) * (len(extent) - dim - 1))

    level = one(*cuts[0])
    for cut in cuts[1:]:
        level = level * one(*cut)
    return level


def normal_values(key, shape, scale, reach, shards=(), kind=jnp.bfloat16):
    values = jax.random.normal(key, shape, jnp.float32) * scale
    if len(shards) > 0:
        values = shard_levels(key, shape, shards, -0.22, 0.18) * values
    return jnp.clip(values, min=-reach, max=reach).astype(kind)


def noise_with(stream_key, extent, spread, most, cuts, heavy, held_as=jnp.bfloat16):
    entries = spread * jax.random.normal(stream_key, extent, jnp.float32)
    if cuts:
        entries = entries * shard_levels(stream_key, extent, cuts, -0.22, 0.18)
    return jnp.clip(spiked(entries, jax.random.fold_in(stream_key, 3), *heavy), -most, most).astype(held_as)


def setup_inputs(seed: int = 0, part: int = 0) -> dict:
    seeds = jax.random.split(jax.random.key(seed), 8)
    own_keys = jax.random.split(jax.random.fold_in(seeds[7], part), 8)
    tokens = noise_with(own_keys[0], (TOKENS, D), 1.0, 6.0, ((0, 16),), (0, 1, 16, 2.0))
    grad_out = normal_values(own_keys[1], (TOKENS, D), 0.5, 3.0, ((0, 16),))
    expert_ids = draw_expert_ids(jax.random.fold_in(jax.random.fold_in(seeds[7], part), 71), part)
    router_weight = normal_values(seeds[3], (D, EXPERTS), D ** -0.5, 0.125)
    gate_weight = normal_values(seeds[4], (2 * EXPERTS, D, FF // 2), D ** -0.5, 0.125, ((0, 16),))
    up_weight = normal_values(seeds[5], (2 * EXPERTS, D, FF // 2), D ** -0.5, 0.125, ((0, 16),))
    down_weight = normal_values(seeds[6], (2 * EXPERTS, FF // 2, D), FF ** -0.5, 0.21875, ((0, 16),))
    return dict(tokens=tokens, grad_out=grad_out, expert_ids=expert_ids, router_weight=router_weight, gate_weight=gate_weight, up_weight=up_weight, down_weight=down_weight)


def expert_pass(rows, grads, gate_full, up_full, down_full):
    pre_gate = jnp.dot(rows, gate_full, preferred_element_type=jnp.float32)
    pre_up = jnp.dot(rows, up_full, preferred_element_type=jnp.float32)
    squash = jax.nn.sigmoid(pre_gate)
    activated = pre_gate * squash
    hidden = (activated * pre_up).astype(jnp.bfloat16)
    partial_out = jnp.dot(hidden, down_full, preferred_element_type=jnp.float32)
    back_hidden = jnp.dot(grads, down_full.T, preferred_element_type=jnp.float32)
    gate_delta = (back_hidden * pre_up * squash * (1.0 + pre_gate * (1.0 - squash))).astype(jnp.bfloat16)
    up_delta = (back_hidden * activated).astype(jnp.bfloat16)
    partial_back = jnp.dot(gate_delta, gate_full.T, preferred_element_type=jnp.float32)
    partial_back = partial_back + jnp.dot(up_delta, up_full.T, preferred_element_type=jnp.float32)
    return partial_out, partial_back, hidden, gate_delta, up_delta


def reference(tokens, grad_out, expert_ids, router_weight, gate_weight, up_weight, down_weight):
    token_total, model_width = tokens.shape
    per_token = expert_ids.shape[1]
    experts = router_weight.shape[1]
    halfway = token_total // N_EXPERT // 2
    pair_count = token_total * per_token
    capacity = CAP_PEER * N_EXPERT
    onehot = expert_ids[:, :, None] == jnp.arange(experts, dtype=jnp.int32)[None, None, :]
    logits = jnp.dot(tokens, router_weight, preferred_element_type=jnp.float32)
    chosen = jnp.sum(jnp.where(onehot, logits[:, None, :], 0.0), axis=2)
    probability = jax.nn.sigmoid(chosen)
    summed = jnp.sum(probability, axis=1, keepdims=True)
    gate_share = probability / summed
    scaled = (gate_share[:, :, None] * grad_out[:, None, :].astype(jnp.float32)).astype(jnp.bfloat16)
    scaled = scaled.reshape(pair_count, model_width)
    parity = (jnp.arange(token_total, dtype=jnp.int32) // halfway) % 2
    group = (2 * expert_ids + parity[:, None]).reshape(pair_count).astype(jnp.int32)
    order = jnp.argsort(group, stable=True).astype(jnp.int32)
    sizes = jnp.bincount(group, length=2 * experts).astype(jnp.int32)
    starts = (jnp.cumsum(sizes) - sizes).astype(jnp.int32)
    slot_index = jnp.arange(capacity, dtype=jnp.int32)

    def one_group(which):
        place = starts[which] + slot_index
        valid = slot_index < sizes[which]
        pick = order[jnp.minimum(place, pair_count - 1)]
        rows = jnp.where(valid[:, None], tokens[pick // per_token], 0.0).astype(tokens.dtype)
        grads = jnp.where(valid[:, None], scaled[pick], 0.0).astype(scaled.dtype)
        return rows, grads, jnp.where(valid, pick, pair_count).astype(jnp.int32)

    def one_expert(expert):
        gate_full = jnp.concatenate([gate_weight[2 * expert], gate_weight[2 * expert + 1]], axis=1)
        up_full = jnp.concatenate([up_weight[2 * expert], up_weight[2 * expert + 1]], axis=1)
        down_full = jnp.concatenate([down_weight[2 * expert], down_weight[2 * expert + 1]], axis=0)
        outs_list, backs_list, picks_list = [], [], []
        gate_sum, up_sum, down_sum = 0.0, 0.0, 0.0
        for which in range(2):
            rows, grads, picks = one_group(2 * expert + which)
            partial_out, partial_back, hidden, gate_delta, up_delta = expert_pass(rows, grads, gate_full, up_full, down_full)
            outs_list.append(partial_out.astype(jnp.bfloat16))
            backs_list.append(partial_back.astype(jnp.bfloat16))
            picks_list.append(picks)
            gate_sum = gate_sum + jnp.dot(rows.T, gate_delta, preferred_element_type=jnp.float32).astype(jnp.bfloat16).astype(jnp.float32)
            up_sum = up_sum + jnp.dot(rows.T, up_delta, preferred_element_type=jnp.float32).astype(jnp.bfloat16).astype(jnp.float32)
            down_sum = down_sum + jnp.dot(hidden.T, grads, preferred_element_type=jnp.float32).astype(jnp.bfloat16).astype(jnp.float32)
        return (jnp.stack(outs_list), jnp.stack(backs_list), jnp.stack(picks_list),
                gate_sum.astype(jnp.bfloat16), up_sum.astype(jnp.bfloat16), down_sum.astype(jnp.bfloat16))

    outs_all, backs_all, picks_all, gate_all, up_all, down_all = lax.map(one_expert, jnp.arange(experts, dtype=jnp.int32))
    flat_picks = picks_all.reshape(-1)
    out_flat = jnp.zeros((pair_count + 1, model_width), outs_all.dtype).at[flat_picks].set(outs_all.reshape(-1, model_width))[:pair_count]
    back_flat = jnp.zeros((pair_count + 1, model_width), backs_all.dtype).at[flat_picks].set(backs_all.reshape(-1, model_width))[:pair_count]
    expert_out = out_flat.reshape(token_total, per_token, model_width).astype(jnp.float32)
    expert_back = back_flat.reshape(token_total, per_token, model_width).astype(jnp.float32)
    mixed = jnp.sum(gate_share[:, :, None] * expert_out, axis=1).astype(jnp.bfloat16)
    gate_slope = jnp.sum(grad_out[:, None, :].astype(jnp.float32) * expert_out, axis=2)
    prob_slope = (gate_slope - jnp.sum(gate_share * gate_slope, axis=1, keepdims=True)) / summed
    logit_slope = prob_slope * probability * (1.0 - probability)
    router_delta = jnp.sum(jnp.where(onehot, logit_slope[:, :, None], 0.0), axis=1).astype(jnp.bfloat16)
    token_grad = jnp.sum(expert_back, axis=1) + jnp.dot(router_delta, router_weight.T, preferred_element_type=jnp.float32)
    token_grad = token_grad.astype(jnp.bfloat16)
    router_grad = jnp.dot(tokens.T, router_delta, preferred_element_type=jnp.float32)
    half_ff = gate_weight.shape[2]
    gate_grad = gate_all.reshape(experts, model_width, 2, half_ff).transpose(0, 2, 1, 3).reshape(2 * experts, model_width, half_ff)
    up_grad = up_all.reshape(experts, model_width, 2, half_ff).transpose(0, 2, 1, 3).reshape(2 * experts, model_width, half_ff)
    down_grad = down_all.reshape(2 * experts, half_ff, model_width)
    return mixed, token_grad, gate_grad, up_grad, down_grad, router_grad
```

```python
import jax
import jax.numpy as jnp
from jax import lax
from jax.sharding import PartitionSpec as P

F32 = jnp.float32
BF16 = jnp.bfloat16


def from_partner(value, axis, distance):
    mask = 2**distance
    pairs = [(source, source ^ mask) for source in range(lax.axis_size(axis))]
    return lax.ppermute(value, axis, pairs)


def dot(left, right):
    return jnp.dot(left, right, preferred_element_type=F32)


def dot_nt(left, right):
    return lax.dot_general(left, right, (((1,), (1,)), ((), ())), preferred_element_type=F32)


def dot_tn(left, right):
    return lax.dot_general(left, right, (((0,), (0,)), ((), ())), preferred_element_type=F32)


def ring_chips(chips):
    return list(range(0, chips, 2)) + list(range(chips - 1, 0, -2))


def ring_send(value, step):
    chips = lax.axis_size("expert") // 2
    ring = ring_chips(chips)
    pairs = [
        (2 * ring[place] + core, 2 * ring[(place + step) % chips] + core)
        for place in range(chips)
        for core in range(2)
    ]
    return lax.ppermute(value, "expert", pairs)


def ring_gather(block, chips):
    far = chips // 2
    half = block.shape[0] // 2
    behind, ahead = [block], [block]
    for _ in range(far - 1):
        behind.append(ring_send(behind[-1], 1))
        ahead.append(ring_send(ahead[-1], -1))
    upper = ring_send(behind[-1][:half], 1)
    lower = ring_send(ahead[-1][half:], -1)
    return behind + [upper, lower] + ahead[:0:-1]


def ring_scatter(terms, chips):
    far = chips // 2
    half = terms(0).shape[0] // 2
    total = terms(0).astype(F32)
    for step, span in ((1, slice(0, half)), (-1, slice(half, 2 * half))):
        moving = ring_send(terms(far)[span], step)
        for distance in range(far - 1, 0, -1):
            own = terms((-step * distance) % chips).astype(F32)
            if distance == far - 1:
                joined = own[span] + moving.astype(F32)
                own = jnp.concatenate([joined, own[half:]] if step == 1 else [own[:half], joined])
            else:
                own = own + moving.astype(F32)
            moving = ring_send(own.astype(BF16), step)
        total = total + moving.astype(F32)
    return total


def all_tokens_pass(
    tokens, grad_out, expert_ids, router_weight, gate_weight, up_weight, down_weight
):
    chips = lax.axis_size("expert") // 2
    rows_own, model_width = tokens.shape
    experts = router_weight.shape[1]
    width = gate_weight.shape[2]
    device = lax.axis_index("expert")
    chip, core = device // 2, device % 2
    place = jnp.where(chip % 2 == 0, chip // 2, chips - 1 - chip // 2)

    def around(array, axis):
        turned = jnp.concatenate(
            [lax.slice_in_dim(array, 0, 1, axis=axis)]
            + [lax.slice_in_dim(array, c, c + 1, axis=axis) for c in range(chips - 1, 0, -1)],
            axis=axis,
        )
        twice = jnp.concatenate([turned, turned], axis=axis)
        return lax.dynamic_slice_in_dim(twice, chips - place, chips, axis=axis)

    token_blocks = ring_gather(tokens, chips)
    grad_blocks = ring_gather(grad_out, chips)

    onehot = (
        expert_ids[:, :, None] == jnp.arange(experts, dtype=jnp.int32)[None, None, :]
    ).astype(F32)
    named = jnp.sum(onehot, axis=1)
    probability = named * jax.nn.sigmoid(dot(tokens, router_weight))
    summed = jnp.sum(probability, axis=1, keepdims=True)
    shares = jnp.concatenate(
        [probability / summed, probability * (1.0 - probability) / summed], axis=1
    )
    shares_all = lax.all_gather(shares, "expert").reshape(chips, 2, rows_own, 2 * experts)
    shares_all = lax.dynamic_index_in_dim(shares_all, core, 1, keepdims=False)
    shares_all = jnp.stack([shares_all[c] for c in ring_chips(chips)])
    shares_all = around(shares_all, 0).reshape(chips * rows_own, 2 * experts)
    gates_all, slope_all = shares_all[:, :experts], shares_all[:, experts:]
    gate_mine = lax.dynamic_slice_in_dim(gates_all, chip, 1, axis=1)

    gate_own, up_own, down_own = gate_weight[0], up_weight[0], down_weight[0]
    gate_other, up_other, down_other = from_partner((gate_own, up_own, down_own), "expert", 0)
    weight_in = jnp.concatenate([gate_own, up_own, gate_other, up_other], axis=1)
    weight_out = jnp.concatenate([down_own, down_other], axis=0)

    rows = jnp.concatenate(token_blocks, axis=0)
    before = dot(rows, weight_in)
    pre_gate = jnp.concatenate([before[:, :width], before[:, 2 * width : 3 * width]], axis=1)
    pre_up = jnp.concatenate([before[:, width : 2 * width], before[:, 3 * width :]], axis=1)
    squash = jax.nn.sigmoid(pre_gate)
    activated = pre_gate * squash
    hidden = activated * pre_up
    hidden_gated = (gate_mine * hidden).astype(BF16)
    out = dot(hidden_gated, weight_out).astype(BF16)

    def block_of(array):
        return lambda j: array[j * rows_own : (j + 1) * rows_own]

    mixed = ring_scatter(block_of(out), chips).astype(BF16)

    grads = jnp.concatenate(grad_blocks, axis=0)
    back_hidden = dot_nt(grads, weight_out)
    gate_slope = jnp.sum(hidden * back_hidden, axis=1)
    back_gated = gate_mine * back_hidden
    gate_delta = (back_gated * pre_up * squash * (1.0 + pre_gate * (1.0 - squash))).astype(BF16)
    up_delta = (back_gated * activated).astype(BF16)
    delta_own = jnp.concatenate([gate_delta[:, :width], up_delta[:, :width]], axis=1)
    delta_other = jnp.concatenate([gate_delta[:, width:], up_delta[:, width:]], axis=1)
    back = dot_nt(jnp.concatenate([delta_own, delta_other], axis=1), weight_in).astype(BF16)
    back_sum = ring_scatter(block_of(back), chips)

    in_other = from_partner(dot_tn(rows, delta_other).astype(BF16), "expert", 0).astype(F32)
    down_other_part = from_partner(
        dot_tn(hidden_gated[:, width:], grads).astype(BF16), "expert", 0
    ).astype(F32)
    in_own = dot_tn(rows, delta_own)
    gate_grad = (in_own[:, :width] + in_other[:, :width]).astype(BF16)[None]
    up_grad = (in_own[:, width:] + in_other[:, width:]).astype(BF16)[None]
    down_grad = (dot_tn(hidden_gated[:, :width], grads) + down_other_part).astype(BF16)[None]

    gate_slope = around(gate_slope.reshape(chips, rows_own), 0)
    slopes = lax.all_gather(gate_slope, "expert").reshape(chips, 2, chips, rows_own)
    slopes = lax.dynamic_index_in_dim(slopes, core, 1, keepdims=False)
    slopes = around(slopes, 1).reshape(chips, chips * rows_own).T
    router_delta = (
        slope_all * (slopes - jnp.sum(gates_all * slopes, axis=1, keepdims=True))
    ).astype(BF16)
    token_grad = (back_sum + dot_nt(router_delta[:rows_own], router_weight)).astype(BF16)
    part = model_width // (2 * chips)
    columns = lax.dynamic_slice_in_dim(rows, chip * 2 * part, 2 * part, axis=1)
    router_part = dot_tn(columns, router_delta).reshape(2, part, experts)
    router_grad = lax.dynamic_index_in_dim(
        router_part, core, 0, keepdims=False
    ) + from_partner(
        lax.dynamic_index_in_dim(router_part, 1 - core, 0, keepdims=False), "expert", 0
    )
    return (mixed, token_grad, gate_grad, up_grad, down_grad, router_grad)


def expert_pass(rows, grads, gate_full, up_full, down_full):
    pre_gate = dot(rows, gate_full)
    pre_up = dot(rows, up_full)
    squash = jax.nn.sigmoid(pre_gate)
    activated = pre_gate * squash
    hidden = (activated * pre_up).astype(BF16)
    partial_out = dot(hidden, down_full)
    back_hidden = dot_nt(grads, down_full)
    gate_delta = (back_hidden * pre_up * squash * (1.0 + pre_gate * (1.0 - squash))).astype(BF16)
    up_delta = (back_hidden * activated).astype(BF16)
    partial_back = dot_nt(gate_delta, gate_full) + dot_nt(up_delta, up_full)
    return (partial_out, partial_back, hidden, gate_delta, up_delta)


def rounded_term(left, right):
    return dot_tn(left, right).astype(BF16).astype(F32)


def slots_pass(tokens, grad_out, expert_ids, router_weight, gate_weight, up_weight, down_weight):
    devices = lax.axis_size("expert")
    token_count, model_width = tokens.shape
    per_token = expert_ids.shape[1]
    experts = router_weight.shape[1]
    halfway = token_count // 2
    capacity = 2 * token_count * per_token // devices
    slot_total = devices * capacity
    pair_count = token_count * per_token
    onehot = expert_ids[:, :, None] == jnp.arange(experts, dtype=jnp.int32)[None, None, :]
    logits = dot(tokens, router_weight)
    chosen = jnp.sum(jnp.where(onehot, logits[:, None, :], 0.0), axis=2)
    probability = jax.nn.sigmoid(chosen)
    summed = jnp.sum(probability, axis=1, keepdims=True)
    gate_share = probability / summed
    scaled = (gate_share[:, :, None] * grad_out[:, None, :].astype(F32)).astype(BF16)
    scaled = scaled.reshape(pair_count, model_width)
    named = jnp.sum(onehot.astype(BF16), axis=1).reshape(2, halfway, experts)
    order = jnp.arange(halfway, dtype=jnp.int32)
    earlier = (order[None, :] < order[:, None]).astype(BF16)
    before = jnp.einsum("st,pte->pse", earlier, named, preferred_element_type=F32)
    before = before.reshape(token_count, 1, experts)
    position = jnp.sum(jnp.where(onehot, before, 0.0), axis=2).astype(jnp.int32)
    parity = (jnp.arange(token_count, dtype=jnp.int32) // halfway)[:, None]
    target = ((2 * expert_ids + parity) * capacity + position).reshape(pair_count)
    source = (
        jnp.full((slot_total,), pair_count, jnp.int32)
        .at[target]
        .set(jnp.arange(pair_count, dtype=jnp.int32))
    )
    filled = (source < pair_count)[:, None]
    clipped = jnp.minimum(source, pair_count - 1)
    row_buffer = jnp.where(filled, jnp.take(tokens, clipped // per_token, axis=0), 0.0)
    grad_buffer = jnp.where(filled, jnp.take(scaled, clipped, axis=0), 0.0)
    row_buffer = row_buffer.reshape(devices, capacity, model_width)
    grad_buffer = grad_buffer.reshape(devices, capacity, model_width)

    def exchange(value):
        return lax.all_to_all(value, "expert", split_axis=0, concat_axis=0, tiled=True)

    rows_in = exchange(row_buffer).reshape(slot_total, model_width)
    grads_in = exchange(grad_buffer).reshape(slot_total, model_width)
    other_rows, other_grads = from_partner((rows_in, grads_in), "expert", 0)
    both_rows = jnp.concatenate([rows_in, other_rows], axis=0)
    both_grads = jnp.concatenate([grads_in, other_grads], axis=0)
    partial_out, partial_back, hidden, gate_delta, up_delta = expert_pass(
        both_rows, both_grads, gate_weight[0], up_weight[0], down_weight[0]
    )
    got_out = from_partner(partial_out[slot_total:].astype(BF16), "expert", 0).astype(F32)
    got_back = from_partner(partial_back[slot_total:].astype(BF16), "expert", 0).astype(F32)
    out_rows = (partial_out[:slot_total] + got_out).astype(BF16)
    back_rows = (partial_back[:slot_total] + got_back).astype(BF16)
    gate_sum = rounded_term(rows_in, gate_delta[:slot_total]) + rounded_term(
        other_rows, gate_delta[slot_total:]
    )
    up_sum = rounded_term(rows_in, up_delta[:slot_total]) + rounded_term(
        other_rows, up_delta[slot_total:]
    )
    down_sum = rounded_term(hidden[:slot_total], grads_in) + rounded_term(
        hidden[slot_total:], other_grads
    )
    gate_grad = gate_sum.astype(BF16)[None]
    up_grad = up_sum.astype(BF16)[None]
    down_grad = down_sum.astype(BF16)[None]
    out_back = exchange(out_rows.reshape(devices, capacity, model_width))
    grad_back = exchange(back_rows.reshape(devices, capacity, model_width))
    expert_out = jnp.take(out_back.reshape(slot_total, model_width), target, axis=0)
    expert_out = expert_out.reshape(token_count, per_token, model_width).astype(F32)
    expert_back = jnp.take(grad_back.reshape(slot_total, model_width), target, axis=0)
    expert_back = expert_back.reshape(token_count, per_token, model_width).astype(F32)
    mixed = jnp.sum(gate_share[:, :, None] * expert_out, axis=1).astype(BF16)
    gate_slope = jnp.sum(grad_out[:, None, :].astype(F32) * expert_out, axis=2)
    prob_slope = (gate_slope - jnp.sum(gate_share * gate_slope, axis=1, keepdims=True)) / summed
    logit_slope = prob_slope * probability * (1.0 - probability)
    router_delta = jnp.sum(jnp.where(onehot, logit_slope[:, :, None], 0.0), axis=1).astype(BF16)
    token_grad = jnp.sum(expert_back, axis=1) + dot_nt(router_delta, router_weight)
    token_grad = token_grad.astype(BF16)
    router_grad = lax.psum_scatter(
        dot_tn(tokens, router_delta), "expert", scatter_dimension=0, tiled=True
    )
    return (mixed, token_grad, gate_grad, up_grad, down_grad, router_grad)


def on_device(tokens, grad_out, expert_ids, router_weight, gate_weight, up_weight, down_weight):
    token_count = tokens.shape[0]
    capacity = 2 * token_count * expert_ids.shape[1] // lax.axis_size("expert")
    step = all_tokens_pass if 2 * capacity >= token_count else slots_pass
    return step(tokens, grad_out, expert_ids, router_weight, gate_weight, up_weight, down_weight)


def solution(mesh):
    return jax.shard_map(
        on_device,
        mesh=mesh,
        in_specs=(
            P(("groups", "expert"), None),
            P(("groups", "expert"), None),
            P(("groups", "expert"), None),
            P(),
            P("expert", None, None),
            P("expert", None, None),
            P("expert", None, None),
        ),
        out_specs=(
            P(("groups", "expert"), None),
            P(("groups", "expert"), None),
            P(("groups", "expert"), None, None),
            P(("groups", "expert"), None, None),
            P(("groups", "expert"), None, None),
            P(("groups", "expert"), None),
        ),
        check_vma=False,
    )
```

```python
import jax
import jax.numpy as jnp
from jax import lax
from jax.experimental import pallas as pl
from jax.experimental.pallas import tpu as pltpu
from jax.sharding import PartitionSpec as P

F32 = jnp.float32
BF16 = jnp.bfloat16


def from_partner(value, axis, distance):
    mask = 2**distance
    pairs = [(source, source ^ mask) for source in range(lax.axis_size(axis))]
    return lax.ppermute(value, axis, pairs)


def dot(left, right):
    return jnp.dot(left, right, preferred_element_type=F32)


def dot_nt(left, right):
    return lax.dot_general(left, right, (((1,), (1,)), ((), ())), preferred_element_type=F32)


def dot_tn(left, right):
    return lax.dot_general(left, right, (((0,), (0,)), ((), ())), preferred_element_type=F32)


LANES = 128
PIECES = 3
MIB = 2**20


def ring_send(value, step):
    chips = lax.axis_size("expert") // 2
    ring = list(range(0, chips, 2)) + list(range(chips - 1, 0, -2))
    pairs = [
        (2 * ring[place] + core, 2 * ring[(place + step) % chips] + core)
        for place in range(chips)
        for core in range(2)
    ]
    return lax.ppermute(value, "expert", pairs)


def after(values, *firsts):
    return lax.optimization_barrier((values, firsts))[0]


def kernel_call(body, name, outs, ins, scratch=(), flops=0, limit=8, **more):
    moved = sum(a.size * a.dtype.itemsize for a in (*ins, *outs))
    return pl.pallas_call(
        body,
        name=name,
        out_shape=outs,
        scratch_shapes=scratch,
        compiler_params=pltpu.CompilerParams(vmem_limit_bytes=limit * MIB),
        cost_estimate=pl.CostEstimate(flops=flops, bytes_accessed=moved, transcendentals=0),
        **more,
    )(*ins)


VMEM = pl.BlockSpec(memory_space=pltpu.VMEM)
ANY = pl.BlockSpec(memory_space=pl.ANY)


def lane_ids(rows):
    return lax.broadcasted_iota(jnp.int32, (rows, LANES), 1)


def pack_block(tokens, grad_out, ids):
    count, width = tokens.shape

    def body(tokens_ref, grads_ref, ids_ref, block_ref):
        block_ref[:, :width] = tokens_ref[...]
        block_ref[:, width : 2 * width] = grads_ref[...]
        block_ref[:, 2 * width :] = ids_ref[...]

    out = jax.ShapeDtypeStruct((count, 2 * width + LANES), BF16)
    return kernel_call(body, "pack_block", (out,), (tokens, grad_out, ids))[0]


def pack_weights(own, other):
    depth, width = own[0].shape
    steps = 4
    tile = depth // steps

    def body(gate_ref, up_ref, down_ref, gate_other_ref, up_other_ref, down_other_ref, in_ref, out_ref):
        for i, ref in enumerate((gate_ref, gate_other_ref, up_ref, up_other_ref)):
            in_ref[:, i * width : (i + 1) * width] = ref[...]
        out_ref[:width] = down_ref[...]
        out_ref[width:] = down_other_ref[...]

    in_spec = pl.BlockSpec((tile, width), lambda d: (d, 0))
    down_spec = pl.BlockSpec((width, tile), lambda d: (0, d))
    return kernel_call(
        body,
        "pack_weights",
        (
            jax.ShapeDtypeStruct((depth, 4 * width), BF16),
            jax.ShapeDtypeStruct((2 * width, depth), BF16),
        ),
        (*own, *other),
        grid=(steps,),
        in_specs=[in_spec, in_spec, down_spec] * 2,
        out_specs=[
            pl.BlockSpec((tile, 4 * width), lambda d: (d, 0)),
            pl.BlockSpec((2 * width, tile), lambda d: (0, d)),
        ],
        limit=16,
    )


def expert_chunk(blocks, weights, router, behind, where, per_token, part):
    number = len(blocks)
    stride = blocks[0].shape[1]
    spans, total = [], 0
    for block in blocks:
        spans.append(slice(total, total + block.shape[0]))
        total += block.shape[0]
    width, model_width = weights[1].shape[0] // 2, weights[1].shape[1]

    def body(*refs):
        block_refs, refs = refs[:number], refs[number:]
        in_ref, down_ref, router_ref, behind_ref, where_ref = refs[:5]
        made_refs, refs = refs[5 : 5 + number], refs[5 + number :]
        hidden_refs, delta_refs = refs[:2], refs[2:4]
        side_ref, column_ref, both_ref, delta_ref = refs[4:]
        for i in range(number):
            both_ref[spans[i], :] = block_refs[i][...]
        rows = both_ref[:, :model_width]
        grads = both_ref[:, model_width : 2 * model_width]
        ids = both_ref[:, 2 * model_width :].astype(F32)
        logits = dot(rows, router_ref[...])
        named = jnp.zeros((total, LANES), F32)
        for k in range(per_token):
            named = named + jnp.where(ids[:, k : k + 1] == behind_ref[...], 1.0, 0.0)
        probability = named * jax.nn.sigmoid(logits)
        summed = jnp.sum(probability, axis=1, keepdims=True)
        gates = probability / summed
        side_ref[:, :LANES] = gates
        side_ref[:, LANES : 2 * LANES] = probability * (1.0 - probability) / summed
        gate = gates[:, :1]
        first = pl.multiple_of(where_ref[0] * 2 * part, 2 * part)
        column_ref[...] = both_ref[:, pl.ds(first, 2 * part)]
        before = dot(rows, in_ref[...])
        pre_gate, pre_up = before[:, : 2 * width], before[:, 2 * width :]
        squash = jax.nn.sigmoid(pre_gate)
        activated = pre_gate * squash
        hidden = activated * pre_up
        hidden_gated = (gate * hidden).astype(BF16)
        back_hidden = dot_nt(grads, down_ref[...])
        slope = jnp.sum(hidden * back_hidden, axis=1, keepdims=True)
        side_ref[:, 2 * LANES :] = jnp.broadcast_to(slope, (total, LANES))
        back_hidden = gate * back_hidden
        gate_delta = back_hidden * pre_up * squash * (1.0 + pre_gate * (1.0 - squash))
        gate_delta, up_delta = gate_delta.astype(BF16), (back_hidden * activated).astype(BF16)
        delta_ref[:, : 2 * width] = gate_delta
        delta_ref[:, 2 * width :] = up_delta
        for h in range(2):
            half = slice(h * width, (h + 1) * width)
            hidden_refs[h][...] = hidden_gated[:, half]
            delta_refs[h][:, :width] = gate_delta[:, half]
            delta_refs[h][:, width:] = up_delta[:, half]
        out = dot(hidden_gated, down_ref[...]).astype(BF16)
        back = dot_nt(delta_ref[...], in_ref[...]).astype(BF16)
        for i in range(number):
            made_refs[i][:, :model_width] = out[spans[i]]
            made_refs[i][:, model_width:] = back[spans[i]]

    outs = (
        *(jax.ShapeDtypeStruct((block.shape[0], 2 * model_width), BF16) for block in blocks),
        *(jax.ShapeDtypeStruct((total, width), BF16) for _ in range(2)),
        *(jax.ShapeDtypeStruct((total, 2 * width), BF16) for _ in range(2)),
        jax.ShapeDtypeStruct((total, 3 * LANES), F32),
        jax.ShapeDtypeStruct((total, 2 * part), BF16),
        jax.ShapeDtypeStruct((total, stride), BF16),
    )
    made = kernel_call(
        body,
        "expert_chunk",
        outs,
        (*blocks, *weights, router, behind, where),
        scratch=[pltpu.VMEM((total, 4 * width), BF16)],
        limit=24,
        flops=24 * total * model_width * width,
        in_specs=[VMEM] * (number + 4) + [pl.BlockSpec(memory_space=pltpu.SMEM)],
        out_specs=[VMEM] * len(outs),
    )
    return made[:number], made[number : number + 2], made[number + 2 : number + 4], made[-3:]


def first_messages(upper, lower, sides, layout):
    half, stride = upper.shape
    count = 2 * half
    chips = len(layout)

    def body(upper_ref, lower_ref, *refs):
        side_refs, (up_ref, down_ref, slopes_ref) = refs[: len(sides)], refs[len(sides) :]
        table = jnp.zeros((count, LANES), F32)
        for k, (index, offset) in enumerate(layout):
            column = side_refs[index][offset : offset + count, :]
            table = jnp.where(lane_ids(count) == k, column, table)
        packed = jnp.zeros((count, LANES), F32)
        for piece in range(PIECES):
            part = table.astype(BF16).astype(F32)
            table = table - part
            packed = packed + (part if piece == 0 else pltpu.roll(part, piece * chips, 1))
        packed = packed[:half] + pltpu.roll(packed[half:], PIECES * chips, 1)
        packed = packed.astype(BF16)
        slopes_ref[...] = packed
        up_ref[:, :stride] = upper_ref[...]
        up_ref[:, stride:] = packed
        down_ref[:, :stride] = lower_ref[...]
        down_ref[:, stride:] = packed

    outs = (
        jax.ShapeDtypeStruct((half, stride + LANES), BF16),
        jax.ShapeDtypeStruct((half, stride + LANES), BF16),
        jax.ShapeDtypeStruct((half, LANES), BF16),
    )
    slope_specs = [pl.BlockSpec((side.shape[0], LANES), lambda i: (0, 2)) for side in sides]
    return kernel_call(
        body,
        "first_messages",
        outs,
        (upper, lower, *sides),
        grid=(1,),
        in_specs=[pl.BlockSpec(upper.shape, lambda i: (0, 0))] * 2 + slope_specs,
        out_specs=[pl.BlockSpec(o.shape, lambda i: (0, 0)) for o in outs],
    )


def next_message(got, made, slopes=None, upper=None, wait_for=()):
    count, stride = made.shape
    half = count // 2
    small = got.shape[0] == half

    def body(got_ref, made_ref, *refs):
        message_ref = refs[-1]
        if small:
            near, rest = (slice(0, half), slice(half, count)) if upper else (slice(half, count), slice(0, half))
            message_ref[near, :stride] = (
                made_ref[near].astype(F32) + got_ref[:, :stride].astype(F32)
            ).astype(BF16)
            message_ref[rest, :stride] = made_ref[rest]
        else:
            message_ref[:, :stride] = (
                made_ref[...].astype(F32) + got_ref[:, :stride].astype(F32)
            ).astype(BF16)
        message_ref[:half, stride:] = refs[0][...] if slopes is not None else got_ref[:half, stride:]
        message_ref[half:, stride:] = jnp.zeros((count - half, LANES), BF16)

    ins = (got, made) if slopes is None else (got, made, slopes)
    out = jax.ShapeDtypeStruct((count, stride + LANES), BF16)
    return kernel_call(
        body,
        "next_message",
        (out,),
        (*ins, *wait_for),
        flops=count * stride,
        in_specs=[VMEM] * len(ins) + [ANY] * len(wait_for),
        out_specs=[VMEM],
    )[0]


def weight_parts(arrived, hidden, delta, half=None, received=None, wait_for=()):
    number = len(arrived)
    total = sum(a.shape[0] for a in arrived)
    model_width = (arrived[0].shape[1] - LANES) // 2
    width = hidden[0].shape[1]
    tile = 256 if model_width % 256 == 0 else model_width
    every = model_width // tile
    steps, skip = (every, 0) if half is None else (every // 2, half * (every // 2))
    chunks = len(hidden)

    def body(*refs):
        token_refs, grad_refs = refs[:number], refs[number : 2 * number]
        hidden_refs = refs[2 * number : 2 * number + chunks]
        delta_refs = refs[2 * number + chunks : 2 * number + 2 * chunks]
        rest = refs[2 * number + 2 * chunks + len(wait_for) : -2]
        hidden_ref, delta_ref = refs[-2:]

        @pl.when(pl.program_id(0) == 0)
        def _():
            first = 0
            for i in range(chunks):
                last = first + hidden_refs[i].shape[0]
                delta_ref[first:last, :] = delta_refs[i][...]
                first = last
            hidden_ref[...] = jnp.concatenate([ref[...] for ref in hidden_refs], axis=0).T

        mark_ref = rest[-1]
        mark_ref[...] = jnp.zeros(mark_ref.shape, F32)
        rows = jnp.concatenate([ref[...] for ref in token_refs], axis=0)
        grads = jnp.concatenate([ref[...] for ref in grad_refs], axis=0)
        into = dot_tn(rows, delta_ref[...])
        down = dot(hidden_ref[...], grads)
        if received is None:
            gate_ref, up_ref, down_ref, _ = rest
            gate_ref[...] = into[:, :width].astype(BF16)
            up_ref[...] = into[:, width:].astype(BF16)
            down_ref[...] = down.astype(BF16)
        else:
            gate_ref, up_ref, down_ref, _ = rest[6:]
            early = pl.program_id(0) < every // 2
            got_gate, got_up, got_down = (
                jnp.where(early, rest[i][...], rest[3 + i][...]).astype(F32) for i in range(3)
            )
            gate_ref[0] = (into[:, :width] + got_gate).astype(BF16)
            up_ref[0] = (into[:, width:] + got_up).astype(BF16)
            down_ref[0] = (down + got_down).astype(BF16)

    def whole(a):
        return pl.BlockSpec(a.shape, lambda d: (0, 0))

    in_specs = [pl.BlockSpec((a.shape[0], tile), lambda d: (0, skip + d)) for a in arrived]
    in_specs += [pl.BlockSpec((a.shape[0], tile), lambda d: (0, every + skip + d)) for a in arrived]
    in_specs += [whole(a) for a in (*hidden, *delta)]
    in_specs += [ANY] * len(wait_for)
    ins = (*arrived, *arrived, *hidden, *delta, *wait_for)
    if received is None:
        shapes = [(model_width // 2, width)] * 2 + [(width, model_width // 2)]
        out_specs = [pl.BlockSpec((tile, width), lambda d: (d, 0))] * 2
        out_specs += [pl.BlockSpec((width, tile), lambda d: (0, d))]
    else:
        shapes = [(1, model_width, width)] * 2 + [(1, width, model_width)]
        out_specs = [pl.BlockSpec((1, tile, width), lambda d: (0, d, 0))] * 2
        out_specs += [pl.BlockSpec((1, width, tile), lambda d: (0, 0, d))]
        last = every // 2 - 1
        in_specs += [pl.BlockSpec((tile, width), lambda d: (jnp.minimum(d, last), 0))] * 2
        in_specs += [pl.BlockSpec((width, tile), lambda d: (0, jnp.minimum(d, last)))]
        in_specs += [pl.BlockSpec((tile, width), lambda d: (jnp.maximum(d - last - 1, 0), 0))] * 2
        in_specs += [pl.BlockSpec((width, tile), lambda d: (0, jnp.maximum(d - last - 1, 0)))]
        ins += received
    outs = [jax.ShapeDtypeStruct(shape, BF16) for shape in shapes]
    outs = (*outs, jax.ShapeDtypeStruct((8, LANES), F32))
    out_specs.append(pl.BlockSpec((8, LANES), lambda d: (0, 0)))
    return kernel_call(
        body,
        "weight_parts",
        outs,
        ins,
        scratch=[pltpu.VMEM((width, total), BF16), pltpu.VMEM((total, 2 * width), BF16)],
        flops=6 * total * tile * steps * width,
        grid=(steps,),
        in_specs=in_specs,
        out_specs=out_specs,
    )


def router_parts(where, pieces, passed, slopes, sides, layout, order, experts, mark):
    chips = len(layout)
    number = len(pieces)
    half, stride = passed[0].shape[0] // 2, passed[0].shape[1]
    count, part = 2 * half, pieces[0].shape[1] // 2

    def body(where_ref, *refs):
        column_refs, refs = refs[:number], refs[number:]
        passed_refs, slopes_ref, refs = refs[: chips - 1], refs[chips - 1], refs[chips:]
        side_refs = refs[: len(sides)]
        delta_ref, keep_ref, send_ref, total_ref = refs[len(sides) + 1 :]
        tables = []
        for k in range(chips):
            packed = (slopes_ref if k == 0 else passed_refs[k - 1])[...].astype(F32)
            halves = []
            for rows in range(2):
                table = jnp.zeros((half, LANES), F32)
                for piece in range(PIECES):
                    first = (PIECES * rows + piece) * chips
                    table = table + (packed if first == 0 else pltpu.roll(packed, LANES - first, 1))
                halves.append(table)
            tables.append(jnp.concatenate(halves, axis=0))
        sub = lax.broadcasted_iota(jnp.int32, (LANES, LANES), 0)
        lane = lane_ids(LANES)
        turn = jnp.zeros((LANES, LANES), F32)
        for k in range(chips):
            turn = jnp.where((sub == k) & (lane == where_ref[2 + k]), 1.0, turn)
        turn = turn.astype(BF16)
        deltas = []
        for q in range(chips):
            slope = jnp.zeros((count, LANES), F32)
            for k in range(chips):
                from_lane = (q - k) % chips
                column = tables[k][:, from_lane : from_lane + 1]
                slope = jnp.where(lane_ids(count) == k, column, slope)
            index, offset = layout[q]
            gates = side_refs[index][offset : offset + count, :LANES]
            factor = side_refs[index][offset : offset + count, LANES : 2 * LANES]
            middle = jnp.sum(gates * slope, axis=1, keepdims=True)
            delta = (factor * (slope - middle)).astype(BF16)
            deltas.append(dot(delta, turn).astype(BF16))
        delta_ref[...] = deltas[0]
        columns = jnp.concatenate([ref[...] for ref in column_refs], axis=0)
        total_ref[...] = dot_tn(columns, jnp.concatenate([deltas[q] for q in order], axis=0))
        core = where_ref[1]
        own, other = pl.multiple_of(core * part, part), pl.multiple_of((1 - core) * part, part)
        keep_ref[...] = total_ref[pl.ds(own, part), :experts]
        send_ref[...] = total_ref[pl.ds(other, part), :experts]

    info = stride // LANES - 1
    in_specs = [pl.BlockSpec(a.shape, lambda i, w: (0, 0)) for a in pieces]
    in_specs += [pl.BlockSpec((half, LANES), lambda i, w: (0, info)) for _ in range(chips - 1)]
    in_specs += [pl.BlockSpec(slopes.shape, lambda i, w: (0, 0))]
    in_specs += [pl.BlockSpec((side.shape[0], 2 * LANES), lambda i, w: (0, 0)) for side in sides]
    outs = (
        jax.ShapeDtypeStruct((count, LANES), BF16),
        jax.ShapeDtypeStruct((part, experts), F32),
        jax.ShapeDtypeStruct((part, experts), F32),
    )
    in_specs += [ANY]
    ins = (where, *pieces, *passed, slopes, *sides, mark)
    return pl.pallas_call(
        body,
        name="router_parts",
        out_shape=outs,
        grid_spec=pltpu.PrefetchScalarGridSpec(
            num_scalar_prefetch=1,
            grid=(1,),
            in_specs=in_specs,
            out_specs=[pl.BlockSpec(o.shape, lambda i, w: (0, 0)) for o in outs],
            scratch_shapes=[pltpu.VMEM((2 * part, LANES), F32)],
        ),
        compiler_params=pltpu.CompilerParams(vmem_limit_bytes=8 * MIB),
        cost_estimate=pl.CostEstimate(flops=10**7, bytes_accessed=10**6, transcendentals=0),
    )(*ins)


def last_sums(got_up, got_down, made, delta, router):
    count, stride = made.shape
    model_width = stride // 2

    def body(up_ref, down_ref, made_ref, delta_ref, router_ref, mixed_ref, grad_ref):
        total = (
            made_ref[...].astype(F32)
            + up_ref[:, :stride].astype(F32)
            + down_ref[:, :stride].astype(F32)
        )
        mixed_ref[...] = total[:, :model_width].astype(BF16)
        grad_ref[...] = (
            total[:, model_width:] + dot_nt(delta_ref[...], router_ref[...])
        ).astype(BF16)

    out = jax.ShapeDtypeStruct((count, model_width), BF16)
    return kernel_call(body, "last_sums", (out, out), (got_up, got_down, made, delta, router))


def all_tokens_pass(
    tokens, grad_out, expert_ids, router_weight, gate_weight, up_weight, down_weight
):
    chips = lax.axis_size("expert") // 2
    far = chips // 2
    count = tokens.shape[0]
    half = count // 2
    per_token = expert_ids.shape[1]
    experts = router_weight.shape[1]
    device = lax.axis_index("expert")
    chip, core = device // 2, device % 2
    place = jnp.where(chip % 2 == 0, chip // 2, chips - 1 - chip // 2)
    behind = (place - jnp.arange(chips, dtype=jnp.int32)) % chips
    behind = jnp.where(behind < far, 2 * behind, 2 * (chips - 1 - behind) + 1)
    where = jnp.concatenate([jnp.stack([chip, core]).astype(jnp.int32), behind])
    turn = (jnp.arange(experts, dtype=jnp.int32)[:, None] == behind[None, :]).astype(BF16)
    turn = jnp.pad(turn, ((0, 0), (0, LANES - chips)))
    router_turned = dot(router_weight, turn).astype(BF16)
    router_wide = jnp.pad(router_weight, ((0, 0), (0, LANES - experts)))
    behind = jnp.pad(behind.astype(F32), (0, LANES - chips), constant_values=-1.0)[None]

    ids = jnp.pad(expert_ids.astype(BF16), ((0, 0), (0, LANES - per_token)))
    block = pack_block(tokens, grad_out, ids)
    own = after((gate_weight[0], up_weight[0], down_weight[0]), block)
    weights = pack_weights(own, from_partner(own, "expert", 0))

    arrived = {0: block}
    made, layout, order = {}, {}, []
    hidden, delta, sides, columns, kept = ([], []), ([], []), [], [], []
    part = tokens.shape[1] // (2 * chips)

    def work(names):
        terms, hiddens, deltas, (side, column, both) = expert_chunk(
            [arrived[name] for name in names],
            weights,
            router_turned,
            behind,
            where,
            per_token,
            part,
        )
        offset = 0
        for name, term in zip(names, terms):
            made[name], layout[name] = term, (len(sides), offset)
            offset += term.shape[0]
        order.extend(names)
        for h in range(2):
            hidden[h].append(hiddens[h])
            delta[h].append(deltas[h])
        sides.append(side)
        columns.append(column)
        kept.append(both)

    waiting = [0]
    for k in range(1, far):
        arrived[k] = ring_send(arrived[k - 1], 1)
        arrived[chips - k] = ring_send(arrived[(chips - k + 1) % chips], -1)
        waiting += [k, chips - k]
        if k < far - 1:
            work(waiting)
            waiting = []
            if k > 1:
                arrived[k], arrived[chips - k] = after(
                    (arrived[k], arrived[chips - k]), *sides[: k - 1]
                )
    ends = after((arrived[far - 1], arrived[far + 1]), *sides)
    arrived["upper"] = ring_send(ends[0][:half], 1)
    arrived["lower"] = ring_send(ends[1][half:], -1)
    work(waiting + ["upper", "lower"])
    layout[far] = layout["upper"]
    layout = [layout[k] for k in range(chips)]
    order = [far if name == "upper" else name for name in order if name != "lower"]

    up, down, slopes = first_messages(made["upper"], made["lower"], sides, layout)
    up, down = ring_send(up, 1), ring_send(down, -1)
    passed = {chips - 1: down}
    for distance in range(far - 1, 0, -1):
        hops = far - distance
        wait_for = tuple(part[-1] for part in parts) if distance == 1 else ()
        up = next_message(
            up, made[chips - distance], slopes if hops == 1 else None, True, wait_for
        )
        down = next_message(down, made[distance], None, False, wait_for)
        before = (up, down)
        up, down = ring_send(up, 1), ring_send(down, -1)
        passed[hops], passed[chips - 1 - hops] = up, down
        if hops == 1:
            parts = [
                weight_parts(kept, hidden[1], delta[1], half=half_of, wait_for=before)
                for half_of in range(2)
            ]
            got = [from_partner(value, "expert", 0) for part_of in parts for value in part_of[:-1]]
    grads = weight_parts(kept, hidden[0], delta[0], received=tuple(got), wait_for=before)
    gate_grad, up_grad, down_grad = grads[:-1]

    router_delta, keep, send = router_parts(
        where,
        columns,
        [passed[k] for k in range(1, chips)],
        slopes,
        sides,
        layout,
        order,
        experts,
        grads[-1],
    )
    router_grad = keep + from_partner(send, "expert", 0)
    mixed, token_grad = last_sums(up, down, made[0], router_delta, router_wide)
    return (mixed, token_grad, gate_grad, up_grad, down_grad, router_grad)


def expert_pass(rows, grads, gate_full, up_full, down_full):
    pre_gate = dot(rows, gate_full)
    pre_up = dot(rows, up_full)
    squash = jax.nn.sigmoid(pre_gate)
    activated = pre_gate * squash
    hidden = (activated * pre_up).astype(BF16)
    partial_out = dot(hidden, down_full)
    back_hidden = dot_nt(grads, down_full)
    gate_delta = (back_hidden * pre_up * squash * (1.0 + pre_gate * (1.0 - squash))).astype(BF16)
    up_delta = (back_hidden * activated).astype(BF16)
    partial_back = dot_nt(gate_delta, gate_full) + dot_nt(up_delta, up_full)
    return (partial_out, partial_back, hidden, gate_delta, up_delta)


def rounded_term(left, right):
    return dot_tn(left, right).astype(BF16).astype(F32)


def slots_pass(tokens, grad_out, expert_ids, router_weight, gate_weight, up_weight, down_weight):
    devices = lax.axis_size("expert")
    token_count, model_width = tokens.shape
    per_token = expert_ids.shape[1]
    experts = router_weight.shape[1]
    halfway = token_count // 2
    capacity = 2 * token_count * per_token // devices
    slot_total = devices * capacity
    pair_count = token_count * per_token
    onehot = expert_ids[:, :, None] == jnp.arange(experts, dtype=jnp.int32)[None, None, :]
    logits = dot(tokens, router_weight)
    chosen = jnp.sum(jnp.where(onehot, logits[:, None, :], 0.0), axis=2)
    probability = jax.nn.sigmoid(chosen)
    summed = jnp.sum(probability, axis=1, keepdims=True)
    gate_share = probability / summed
    scaled = (gate_share[:, :, None] * grad_out[:, None, :].astype(F32)).astype(BF16)
    scaled = scaled.reshape(pair_count, model_width)
    named = jnp.sum(onehot.astype(BF16), axis=1).reshape(2, halfway, experts)
    order = jnp.arange(halfway, dtype=jnp.int32)
    earlier = (order[None, :] < order[:, None]).astype(BF16)
    before = jnp.einsum("st,pte->pse", earlier, named, preferred_element_type=F32)
    before = before.reshape(token_count, 1, experts)
    position = jnp.sum(jnp.where(onehot, before, 0.0), axis=2).astype(jnp.int32)
    parity = (jnp.arange(token_count, dtype=jnp.int32) // halfway)[:, None]
    target = ((2 * expert_ids + parity) * capacity + position).reshape(pair_count)
    source = (
        jnp.full((slot_total,), pair_count, jnp.int32)
        .at[target]
        .set(jnp.arange(pair_count, dtype=jnp.int32))
    )
    filled = (source < pair_count)[:, None]
    clipped = jnp.minimum(source, pair_count - 1)
    row_buffer = jnp.where(filled, jnp.take(tokens, clipped // per_token, axis=0), 0.0)
    grad_buffer = jnp.where(filled, jnp.take(scaled, clipped, axis=0), 0.0)
    row_buffer = row_buffer.reshape(devices, capacity, model_width)
    grad_buffer = grad_buffer.reshape(devices, capacity, model_width)

    def exchange(value):
        return lax.all_to_all(value, "expert", split_axis=0, concat_axis=0, tiled=True)

    rows_in = exchange(row_buffer).reshape(slot_total, model_width)
    grads_in = exchange(grad_buffer).reshape(slot_total, model_width)
    other_rows, other_grads = from_partner((rows_in, grads_in), "expert", 0)
    both_rows = jnp.concatenate([rows_in, other_rows], axis=0)
    both_grads = jnp.concatenate([grads_in, other_grads], axis=0)
    partial_out, partial_back, hidden, gate_delta, up_delta = expert_pass(
        both_rows, both_grads, gate_weight[0], up_weight[0], down_weight[0]
    )
    got_out = from_partner(partial_out[slot_total:].astype(BF16), "expert", 0).astype(F32)
    got_back = from_partner(partial_back[slot_total:].astype(BF16), "expert", 0).astype(F32)
    out_rows = (partial_out[:slot_total] + got_out).astype(BF16)
    back_rows = (partial_back[:slot_total] + got_back).astype(BF16)
    gate_sum = rounded_term(rows_in, gate_delta[:slot_total]) + rounded_term(
        other_rows, gate_delta[slot_total:]
    )
    up_sum = rounded_term(rows_in, up_delta[:slot_total]) + rounded_term(
        other_rows, up_delta[slot_total:]
    )
    down_sum = rounded_term(hidden[:slot_total], grads_in) + rounded_term(
        hidden[slot_total:], other_grads
    )
    gate_grad = gate_sum.astype(BF16)[None]
    up_grad = up_sum.astype(BF16)[None]
    down_grad = down_sum.astype(BF16)[None]
    out_back = exchange(out_rows.reshape(devices, capacity, model_width))
    grad_back = exchange(back_rows.reshape(devices, capacity, model_width))
    expert_out = jnp.take(out_back.reshape(slot_total, model_width), target, axis=0)
    expert_out = expert_out.reshape(token_count, per_token, model_width).astype(F32)
    expert_back = jnp.take(grad_back.reshape(slot_total, model_width), target, axis=0)
    expert_back = expert_back.reshape(token_count, per_token, model_width).astype(F32)
    mixed = jnp.sum(gate_share[:, :, None] * expert_out, axis=1).astype(BF16)
    gate_slope = jnp.sum(grad_out[:, None, :].astype(F32) * expert_out, axis=2)
    prob_slope = (gate_slope - jnp.sum(gate_share * gate_slope, axis=1, keepdims=True)) / summed
    logit_slope = prob_slope * probability * (1.0 - probability)
    router_delta = jnp.sum(jnp.where(onehot, logit_slope[:, :, None], 0.0), axis=1).astype(BF16)
    token_grad = jnp.sum(expert_back, axis=1) + dot_nt(router_delta, router_weight)
    token_grad = token_grad.astype(BF16)
    router_grad = lax.psum_scatter(
        dot_tn(tokens, router_delta), "expert", scatter_dimension=0, tiled=True
    )
    return (mixed, token_grad, gate_grad, up_grad, down_grad, router_grad)


def on_device(tokens, grad_out, expert_ids, router_weight, gate_weight, up_weight, down_weight):
    token_count = tokens.shape[0]
    capacity = 2 * token_count * expert_ids.shape[1] // lax.axis_size("expert")
    step = all_tokens_pass if 2 * capacity >= token_count else slots_pass
    return step(tokens, grad_out, expert_ids, router_weight, gate_weight, up_weight, down_weight)


def solution(mesh):
    return jax.shard_map(
        on_device,
        mesh=mesh,
        in_specs=(
            P(("groups", "expert"), None),
            P(("groups", "expert"), None),
            P(("groups", "expert"), None),
            P(),
            P("expert", None, None),
            P("expert", None, None),
            P("expert", None, None),
        ),
        out_specs=(
            P(("groups", "expert"), None),
            P(("groups", "expert"), None),
            P(("groups", "expert"), None, None),
            P(("groups", "expert"), None, None),
            P(("groups", "expert"), None, None),
            P(("groups", "expert"), None),
        ),
        check_vma=False,
    )
```

```python
import jax
import jax.numpy as jnp
from jax import lax
from jax.experimental import pallas as pl
from jax.experimental.pallas import tpu as pltpu
from jax.sharding import PartitionSpec as P

F32 = jnp.float32
BF16 = jnp.bfloat16


def from_partner(value, axis, distance):
    mask = 2**distance
    pairs = [(source, source ^ mask) for source in range(lax.axis_size(axis))]
    return lax.ppermute(value, axis, pairs)


def dot(left, right):
    return jnp.dot(left, right, preferred_element_type=F32)


def dot_nt(left, right):
    return lax.dot_general(left, right, (((1,), (1,)), ((), ())), preferred_element_type=F32)


def dot_tn(left, right):
    return lax.dot_general(left, right, (((0,), (0,)), ((), ())), preferred_element_type=F32)


LANES = 128
PIECES = 3
MIB = 2**20


def ring_send(value, step):
    chips = lax.axis_size("expert") // 2
    ring = list(range(0, chips, 2)) + list(range(chips - 1, 0, -2))
    pairs = [
        (2 * ring[place] + core, 2 * ring[(place + step) % chips] + core)
        for place in range(chips)
        for core in range(2)
    ]
    return lax.ppermute(value, "expert", pairs)


def after(values, *firsts):
    return lax.optimization_barrier((values, firsts))[0]


def kernel_call(body, name, outs, ins, scratch=(), flops=0, limit=8, **more):
    moved = sum(a.size * a.dtype.itemsize for a in (*ins, *outs))
    return pl.pallas_call(
        body,
        name=name,
        out_shape=outs,
        scratch_shapes=scratch,
        compiler_params=pltpu.CompilerParams(vmem_limit_bytes=limit * MIB),
        cost_estimate=pl.CostEstimate(flops=flops, bytes_accessed=moved, transcendentals=0),
        **more,
    )(*ins)


VMEM = pl.BlockSpec(memory_space=pltpu.VMEM)
ANY = pl.BlockSpec(memory_space=pl.ANY)


def in_hbm(array):
    return pltpu.with_memory_space_constraint(array, pltpu.HBM)


def lane_ids(rows):
    return lax.broadcasted_iota(jnp.int32, (rows, LANES), 1)


def pack_block(tokens, grad_out, ids):
    count, width = tokens.shape
    per_token = ids.shape[1]

    def body(tokens_ref, grads_ref, ids_hbm, block_ref, ids_ref, sems):
        copies = [
            pltpu.make_async_copy(
                ref, block_ref.at[:, pl.ds(i * width, width)], sems.at[i]
            )
            for i, ref in enumerate((tokens_ref, grads_ref))
        ]
        numbers = pltpu.make_async_copy(ids_hbm, ids_ref, sems.at[2])
        numbers.start()
        for copy in copies:
            copy.start()
        numbers.wait()
        row = lax.broadcasted_iota(jnp.int32, (per_token, LANES), 0)
        spread = (row == lane_ids(per_token)).astype(F32).astype(BF16)
        numbers = ids_ref[...].astype(F32).astype(BF16)
        block_ref[:, 2 * width :] = dot_tn(numbers, spread).astype(BF16)
        for copy in copies:
            copy.wait()

    out = jax.ShapeDtypeStruct((count, 2 * width + LANES), BF16)
    return kernel_call(
        body,
        "pack_block",
        (out,),
        (in_hbm(tokens), in_hbm(grad_out), in_hbm(ids.T)),
        scratch=[pltpu.VMEM((per_token, count), jnp.int32), pltpu.SemaphoreType.DMA((3,))],
        in_specs=[ANY] * 3,
        out_specs=[VMEM],
    )[0]


def pack_weights(own, other):
    depth, width = own[0].shape
    steps = 4
    tile = depth // steps

    def body(gate_ref, up_ref, down_ref, gate_other_ref, up_other_ref, down_other_ref, in_ref, out_ref):
        for i, ref in enumerate((gate_ref, gate_other_ref, up_ref, up_other_ref)):
            in_ref[:, i * width : (i + 1) * width] = ref[...]
        out_ref[:width] = down_ref[...]
        out_ref[width:] = down_other_ref[...]

    in_spec = pl.BlockSpec((tile, width), lambda d: (d, 0))
    down_spec = pl.BlockSpec((width, tile), lambda d: (0, d))
    return kernel_call(
        body,
        "pack_weights",
        (
            jax.ShapeDtypeStruct((depth, 4 * width), BF16),
            jax.ShapeDtypeStruct((2 * width, depth), BF16),
        ),
        (*own, *other),
        grid=(steps,),
        in_specs=[in_spec, in_spec, down_spec] * 2,
        out_specs=[
            pl.BlockSpec((tile, 4 * width), lambda d: (d, 0)),
            pl.BlockSpec((2 * width, tile), lambda d: (0, d)),
        ],
        limit=16,
    )


def expert_chunk(blocks, weights, router, behind, where, per_token, part, wait_for=()):
    number = len(blocks)
    stride = blocks[0].shape[1]
    spans, total = [], 0
    for block in blocks:
        spans.append(slice(total, total + block.shape[0]))
        total += block.shape[0]
    width, model_width = weights[1].shape[0] // 2, weights[1].shape[1]

    def body(*refs):
        block_refs, refs = refs[:number], refs[number:]
        in_ref, down_ref, router_ref, behind_ref, where_ref = refs[:5]
        refs = refs[5 + len(wait_for) :]
        made_refs, refs = refs[:number], refs[number:]
        hidden_refs, delta_refs = refs[:2], refs[2:4]
        side_ref, column_ref, both_ref, delta_ref = refs[4:]
        for i in range(number):
            both_ref[spans[i], :] = block_refs[i][...]
        rows = both_ref[:, :model_width]
        grads = both_ref[:, model_width : 2 * model_width]
        ids = both_ref[:, 2 * model_width :].astype(F32)
        logits = dot(rows, router_ref[...])
        named = jnp.zeros((total, LANES), F32)
        for k in range(per_token):
            named = named + jnp.where(ids[:, k : k + 1] == behind_ref[...], 1.0, 0.0)
        probability = named * jax.nn.sigmoid(logits)
        summed = jnp.sum(probability, axis=1, keepdims=True)
        gates = probability / summed
        side_ref[:, :LANES] = gates
        side_ref[:, LANES : 2 * LANES] = probability * (1.0 - probability) / summed
        gate = gates[:, :1]
        first = pl.multiple_of(where_ref[0] * 2 * part, 2 * part)
        column_ref[...] = both_ref[:, pl.ds(first, 2 * part)]
        before = dot(rows, in_ref[...])
        pre_gate, pre_up = before[:, : 2 * width], before[:, 2 * width :]
        squash = jax.nn.sigmoid(pre_gate)
        activated = pre_gate * squash
        hidden = activated * pre_up
        hidden_gated = (gate * hidden).astype(BF16)
        back_hidden = dot_nt(grads, down_ref[...])
        slope = jnp.sum(hidden * back_hidden, axis=1, keepdims=True)
        side_ref[:, 2 * LANES :] = jnp.broadcast_to(slope, (total, LANES))
        back_hidden = gate * back_hidden
        gate_delta = back_hidden * pre_up * squash * (1.0 + pre_gate * (1.0 - squash))
        gate_delta, up_delta = gate_delta.astype(BF16), (back_hidden * activated).astype(BF16)
        delta_ref[:, : 2 * width] = gate_delta
        delta_ref[:, 2 * width :] = up_delta
        for h in range(2):
            half = slice(h * width, (h + 1) * width)
            hidden_refs[h][...] = hidden_gated[:, half]
            delta_refs[h][:, :width] = gate_delta[:, half]
            delta_refs[h][:, width:] = up_delta[:, half]
        out = dot(hidden_gated, down_ref[...]).astype(BF16)
        back = dot_nt(delta_ref[...], in_ref[...]).astype(BF16)
        for i in range(number):
            made_refs[i][:, :model_width] = out[spans[i]]
            made_refs[i][:, model_width:] = back[spans[i]]

    outs = (
        *(jax.ShapeDtypeStruct((block.shape[0], 2 * model_width), BF16) for block in blocks),
        *(jax.ShapeDtypeStruct((total, width), BF16) for _ in range(2)),
        *(jax.ShapeDtypeStruct((total, 2 * width), BF16) for _ in range(2)),
        jax.ShapeDtypeStruct((total, 3 * LANES), F32),
        jax.ShapeDtypeStruct((total, 2 * part), BF16),
        jax.ShapeDtypeStruct((total, stride), BF16),
    )
    made = kernel_call(
        body,
        "expert_chunk",
        outs,
        (*blocks, *weights, router, behind, where, *wait_for),
        scratch=[pltpu.VMEM((total, 4 * width), BF16)],
        limit=24,
        flops=24 * total * model_width * width,
        in_specs=[VMEM] * (number + 4)
        + [pl.BlockSpec(memory_space=pltpu.SMEM)]
        + [ANY] * len(wait_for),
        out_specs=[VMEM] * len(outs),
    )
    return made[:number], made[number : number + 2], made[number + 2 : number + 4], made[-3:]


def first_messages(upper, lower, sides, layout):
    half, stride = upper.shape
    count = 2 * half
    chips = len(layout)

    def body(upper_ref, lower_ref, *refs):
        side_refs, (up_ref, down_ref, slopes_ref) = refs[: len(sides)], refs[len(sides) :]
        table = jnp.zeros((count, LANES), F32)
        for k, (index, offset) in enumerate(layout):
            column = side_refs[index][offset : offset + count, :]
            table = jnp.where(lane_ids(count) == k, column, table)
        packed = jnp.zeros((count, LANES), F32)
        for piece in range(PIECES):
            part = table.astype(BF16).astype(F32)
            table = table - part
            packed = packed + (part if piece == 0 else pltpu.roll(part, piece * chips, 1))
        packed = packed[:half] + pltpu.roll(packed[half:], PIECES * chips, 1)
        packed = packed.astype(BF16)
        slopes_ref[...] = packed
        up_ref[:, :stride] = upper_ref[...]
        up_ref[:, stride:] = packed
        down_ref[:, :stride] = lower_ref[...]
        down_ref[:, stride:] = packed

    outs = (
        jax.ShapeDtypeStruct((half, stride + LANES), BF16),
        jax.ShapeDtypeStruct((half, stride + LANES), BF16),
        jax.ShapeDtypeStruct((half, LANES), BF16),
    )
    slope_specs = [pl.BlockSpec((side.shape[0], LANES), lambda i: (0, 2)) for side in sides]
    return kernel_call(
        body,
        "first_messages",
        outs,
        (upper, lower, *sides),
        grid=(1,),
        in_specs=[pl.BlockSpec(upper.shape, lambda i: (0, 0))] * 2 + slope_specs,
        out_specs=[pl.BlockSpec(o.shape, lambda i: (0, 0)) for o in outs],
    )


def next_message(got, made, upper, wait_for=()):
    count, stride = made.shape
    half = count // 2
    small = got.shape[0] == half

    def body(got_ref, made_ref, *refs):
        message_ref = refs[-1]
        if small:
            near, rest = (slice(0, half), slice(half, count)) if upper else (slice(half, count), slice(0, half))
            message_ref[near, :stride] = (
                made_ref[near].astype(F32) + got_ref[:, :stride].astype(F32)
            ).astype(BF16)
            message_ref[rest, :stride] = made_ref[rest]
        else:
            message_ref[:, :stride] = (
                made_ref[...].astype(F32) + got_ref[:, :stride].astype(F32)
            ).astype(BF16)
        message_ref[:half, stride:] = got_ref[:half, stride:]
        message_ref[half:, stride:] = jnp.zeros((count - half, LANES), BF16)

    out = jax.ShapeDtypeStruct((count, stride + LANES), BF16)
    return kernel_call(
        body,
        "next_message",
        (out,),
        (got, made, *wait_for),
        flops=count * stride,
        in_specs=[VMEM] * 2 + [ANY] * len(wait_for),
        out_specs=[VMEM],
    )[0]


def weight_parts(arrived, hidden, delta, half=None, received=None, wait_for=()):
    number = len(arrived)
    total = sum(a.shape[0] for a in arrived)
    model_width = (arrived[0].shape[1] - LANES) // 2
    width = hidden[0].shape[1]
    tile = 256 if model_width % 256 == 0 else model_width
    every = model_width // tile
    steps, skip = (every, 0) if half is None else (every // 2, half * (every // 2))
    chunks = len(hidden)

    def body(*refs):
        token_refs, grad_refs = refs[:number], refs[number : 2 * number]
        hidden_refs = refs[2 * number : 2 * number + chunks]
        delta_refs = refs[2 * number + chunks : 2 * number + 2 * chunks]
        rest = refs[2 * number + 2 * chunks + len(wait_for) : -2]
        hidden_ref, delta_ref = refs[-2:]

        @pl.when(pl.program_id(0) == 0)
        def _():
            first = 0
            for i in range(chunks):
                last = first + hidden_refs[i].shape[0]
                delta_ref[first:last, :] = delta_refs[i][...]
                first = last
            hidden_ref[...] = jnp.concatenate([ref[...] for ref in hidden_refs], axis=0).T

        mark_ref = rest[-1]
        mark_ref[...] = jnp.zeros(mark_ref.shape, F32)
        rows = jnp.concatenate([ref[...] for ref in token_refs], axis=0)
        grads = jnp.concatenate([ref[...] for ref in grad_refs], axis=0)
        into = dot_tn(rows, delta_ref[...])
        down = dot(hidden_ref[...], grads)
        if received is None:
            gate_ref, up_ref, down_ref, _ = rest
            gate_ref[...] = into[:, :width].astype(BF16)
            up_ref[...] = into[:, width:].astype(BF16)
            down_ref[...] = down.astype(BF16)
        else:
            gate_ref, up_ref, down_ref, _ = rest[6:]
            early = pl.program_id(0) < every // 2
            got_gate, got_up, got_down = (
                jnp.where(early, rest[i][...], rest[3 + i][...]).astype(F32) for i in range(3)
            )
            gate_ref[0] = (into[:, :width] + got_gate).astype(BF16)
            up_ref[0] = (into[:, width:] + got_up).astype(BF16)
            down_ref[0] = (down + got_down).astype(BF16)

    def whole(a):
        return pl.BlockSpec(a.shape, lambda d: (0, 0))

    in_specs = [pl.BlockSpec((a.shape[0], tile), lambda d: (0, skip + d)) for a in arrived]
    in_specs += [pl.BlockSpec((a.shape[0], tile), lambda d: (0, every + skip + d)) for a in arrived]
    in_specs += [whole(a) for a in (*hidden, *delta)]
    in_specs += [ANY] * len(wait_for)
    ins = (*arrived, *arrived, *hidden, *delta, *wait_for)
    if received is None:
        shapes = [(model_width // 2, width)] * 2 + [(width, model_width // 2)]
        out_specs = [pl.BlockSpec((tile, width), lambda d: (d, 0))] * 2
        out_specs += [pl.BlockSpec((width, tile), lambda d: (0, d))]
    else:
        shapes = [(1, model_width, width)] * 2 + [(1, width, model_width)]
        out_specs = [pl.BlockSpec((1, tile, width), lambda d: (0, d, 0))] * 2
        out_specs += [pl.BlockSpec((1, width, tile), lambda d: (0, 0, d))]
        last = every // 2 - 1
        in_specs += [pl.BlockSpec((tile, width), lambda d: (jnp.minimum(d, last), 0))] * 2
        in_specs += [pl.BlockSpec((width, tile), lambda d: (0, jnp.minimum(d, last)))]
        in_specs += [pl.BlockSpec((tile, width), lambda d: (jnp.maximum(d - last - 1, 0), 0))] * 2
        in_specs += [pl.BlockSpec((width, tile), lambda d: (0, jnp.maximum(d - last - 1, 0)))]
        ins += received
    outs = [jax.ShapeDtypeStruct(shape, BF16) for shape in shapes]
    outs = (*outs, jax.ShapeDtypeStruct((8, LANES), F32))
    out_specs.append(pl.BlockSpec((8, LANES), lambda d: (0, 0)))
    return kernel_call(
        body,
        "weight_parts",
        outs,
        ins,
        scratch=[pltpu.VMEM((width, total), BF16), pltpu.VMEM((total, 2 * width), BF16)],
        flops=6 * total * tile * steps * width,
        grid=(steps,),
        in_specs=in_specs,
        out_specs=out_specs,
    )


def router_parts(where, pieces, passed, slopes, sides, layout, order, experts, mark):
    chips = len(layout)
    number = len(pieces)
    half, part = slopes.shape[0], pieces[0].shape[1] // 2
    count = 2 * half

    def body(where_ref, *refs):
        column_refs, refs = refs[:number], refs[number:]
        passed_refs, slopes_ref, refs = refs[: chips - 1], refs[chips - 1], refs[chips:]
        side_refs = refs[: len(sides)]
        delta_ref, keep_ref, send_ref, total_ref = refs[len(sides) + 1 :]
        tables = []
        for k in range(chips):
            packed = (slopes_ref if k == 0 else passed_refs[k - 1])[...].astype(F32)
            halves = []
            for rows in range(2):
                table = jnp.zeros((half, LANES), F32)
                for piece in range(PIECES):
                    first = (PIECES * rows + piece) * chips
                    table = table + (packed if first == 0 else pltpu.roll(packed, LANES - first, 1))
                halves.append(table)
            tables.append(jnp.concatenate(halves, axis=0))
        sub = lax.broadcasted_iota(jnp.int32, (LANES, LANES), 0)
        lane = lane_ids(LANES)
        turn = jnp.zeros((LANES, LANES), F32)
        for k in range(chips):
            turn = jnp.where((sub == k) & (lane == where_ref[2 + k]), 1.0, turn)
        turn = turn.astype(BF16)
        deltas = []
        for q in range(chips):
            slope = jnp.zeros((count, LANES), F32)
            for k in range(chips):
                from_lane = (q - k) % chips
                column = tables[k][:, from_lane : from_lane + 1]
                slope = jnp.where(lane_ids(count) == k, column, slope)
            index, offset = layout[q]
            gates = side_refs[index][offset : offset + count, :LANES]
            factor = side_refs[index][offset : offset + count, LANES : 2 * LANES]
            middle = jnp.sum(gates * slope, axis=1, keepdims=True)
            deltas.append((factor * (slope - middle)).astype(BF16))
        delta_ref[...] = deltas[0]
        deltas = [dot(delta, turn).astype(BF16) for delta in deltas]
        columns = jnp.concatenate([ref[...] for ref in column_refs], axis=0)
        total_ref[...] = dot_tn(jnp.concatenate([deltas[q] for q in order], axis=0), columns)
        core = where_ref[1]
        own, other = pl.multiple_of(core * part, part), pl.multiple_of((1 - core) * part, part)
        keep_ref[...] = total_ref[:experts, pl.ds(own, part)]
        send_ref[...] = total_ref[:experts, pl.ds(other, part)]

    in_specs = [pl.BlockSpec(a.shape, lambda i, w: (0, 0)) for a in pieces]
    in_specs += [
        pl.BlockSpec((half, LANES), lambda i, w, last=a.shape[1] // LANES - 1: (0, last))
        for a in passed
    ]
    in_specs += [pl.BlockSpec(slopes.shape, lambda i, w: (0, 0))]
    in_specs += [pl.BlockSpec((side.shape[0], 2 * LANES), lambda i, w: (0, 0)) for side in sides]
    outs = (
        jax.ShapeDtypeStruct((count, LANES), BF16),
        jax.ShapeDtypeStruct((experts, part), F32),
        jax.ShapeDtypeStruct((experts, part), F32),
    )
    in_specs += [ANY]
    ins = (where, *pieces, *passed, slopes, *sides, mark)
    return pl.pallas_call(
        body,
        name="router_parts",
        out_shape=outs,
        grid_spec=pltpu.PrefetchScalarGridSpec(
            num_scalar_prefetch=1,
            grid=(1,),
            in_specs=in_specs,
            out_specs=[pl.BlockSpec(o.shape, lambda i, w: (0, 0)) for o in outs],
            scratch_shapes=[pltpu.VMEM((LANES, 2 * part), F32)],
        ),
        compiler_params=pltpu.CompilerParams(vmem_limit_bytes=8 * MIB),
        cost_estimate=pl.CostEstimate(flops=10**7, bytes_accessed=10**6, transcendentals=0),
    )(*ins)


def last_sums(got_up, got_down, made, delta, router):
    count, stride = made.shape
    model_width = stride // 2

    def body(up_ref, down_ref, made_ref, delta_ref, router_ref, mixed_ref, grad_ref):
        total = (
            made_ref[...].astype(F32)
            + up_ref[:, :stride].astype(F32)
            + down_ref[:, :stride].astype(F32)
        )
        mixed_ref[...] = total[:, :model_width].astype(BF16)
        grad_ref[...] = (
            total[:, model_width:] + dot_nt(delta_ref[...], router_ref[...])
        ).astype(BF16)

    out = jax.ShapeDtypeStruct((count, model_width), BF16)
    return kernel_call(body, "last_sums", (out, out), (got_up, got_down, made, delta, router))


def all_tokens_pass(
    tokens, grad_out, expert_ids, router_weight, gate_weight, up_weight, down_weight
):
    chips = lax.axis_size("expert") // 2
    far = chips // 2
    count = tokens.shape[0]
    half = count // 2
    per_token = expert_ids.shape[1]
    experts = router_weight.shape[1]
    device = lax.axis_index("expert")
    chip, core = device // 2, device % 2
    place = jnp.where(chip % 2 == 0, chip // 2, chips - 1 - chip // 2)
    behind = (place - jnp.arange(chips, dtype=jnp.int32)) % chips
    behind = jnp.where(behind < far, 2 * behind, 2 * (chips - 1 - behind) + 1)
    where = jnp.concatenate([jnp.stack([chip, core]).astype(jnp.int32), behind])
    turn = (jnp.arange(experts, dtype=jnp.int32)[:, None] == behind[None, :]).astype(BF16)
    turn = jnp.pad(turn, ((0, 0), (0, LANES - chips)))
    router_turned = dot(router_weight, turn).astype(BF16)
    behind = jnp.pad(behind.astype(F32), (0, LANES - chips), constant_values=-1.0)[None]

    block = pack_block(tokens, grad_out, expert_ids)
    own = after((gate_weight[0], up_weight[0], down_weight[0]), block)
    weights = pack_weights(own, from_partner(own, "expert", 0))

    arrived = {0: block}
    made, layout, order = {}, {}, []
    hidden, delta, sides, columns, kept = ([], []), ([], []), [], [], []
    part = tokens.shape[1] // (2 * chips)

    def work(names):
        terms, hiddens, deltas, (side, column, both) = expert_chunk(
            [arrived[name] for name in names],
            weights,
            router_turned,
            behind,
            where,
            per_token,
            part,
            tuple(sides[-1:]),
        )
        offset = 0
        for name, term in zip(names, terms):
            made[name], layout[name] = term, (len(sides), offset)
            offset += term.shape[0]
        order.extend(names)
        for h in range(2):
            hidden[h].append(hiddens[h])
            delta[h].append(deltas[h])
        sides.append(side)
        columns.append(column)
        kept.append(both)

    waiting = [0]
    for k in range(1, far):
        arrived[k] = ring_send(arrived[k - 1], 1)
        arrived[chips - k] = ring_send(arrived[(chips - k + 1) % chips], -1)
        waiting += [k, chips - k]
        if k == far - 2:
            work(waiting)
            waiting = []
            for name in (k, chips - k):
                arrived[name] = after(arrived[name], *weights)
    ends = [after(arrived[name], *sides) for name in (far - 1, far + 1)]
    arrived["upper"] = ring_send(ends[0][:half], 1)
    arrived["lower"] = ring_send(ends[1][half:], -1)
    work(waiting)
    work(["upper", "lower"])
    layout[far] = layout["upper"]
    layout = [layout[k] for k in range(chips)]
    order = [far if name == "upper" else name for name in order if name != "lower"]

    up, down, slopes = first_messages(made["upper"], made["lower"], sides, layout)
    up, down = ring_send(up, 1), ring_send(down, -1)
    passed = {1: up, chips - 1: down, far: ring_send(slopes, far)}
    for distance in range(far - 1, 0, -1):
        hops = far - distance
        wait_for = ()
        if distance == 1:
            wait_for = tuple(part[-1] for part in parts)
        elif distance == far - 1:
            wait_for = (passed[far],)
        up = next_message(up, made[chips - distance], True, wait_for)
        down = next_message(down, made[distance], False, wait_for)
        before = (up, down)
        up, down = ring_send(up, 1), ring_send(down, -1)
        if distance > 1:
            passed[hops + 1], passed[chips - 1 - hops] = up, down
        if hops == 1:
            parts = [
                weight_parts(kept, hidden[1], delta[1], half=half_of, wait_for=before)
                for half_of in range(2)
            ]
            got = [from_partner(value, "expert", 0) for part_of in parts for value in part_of[:-1]]
    grads = weight_parts(kept, hidden[0], delta[0], received=tuple(got), wait_for=before)
    gate_grad, up_grad, down_grad = grads[:-1]

    router_delta, keep, send = router_parts(
        where,
        columns,
        [passed[k] for k in range(1, chips)],
        slopes,
        sides,
        layout,
        order,
        experts,
        grads[-1],
    )
    router_grad = (keep + from_partner(send, "expert", 0)).T
    mixed, token_grad = last_sums(up, down, made[0], router_delta, router_turned)
    return (mixed, token_grad, gate_grad, up_grad, down_grad, router_grad)


def expert_pass(rows, grads, gate_full, up_full, down_full):
    pre_gate = dot(rows, gate_full)
    pre_up = dot(rows, up_full)
    squash = jax.nn.sigmoid(pre_gate)
    activated = pre_gate * squash
    hidden = (activated * pre_up).astype(BF16)
    partial_out = dot(hidden, down_full)
    back_hidden = dot_nt(grads, down_full)
    gate_delta = (back_hidden * pre_up * squash * (1.0 + pre_gate * (1.0 - squash))).astype(BF16)
    up_delta = (back_hidden * activated).astype(BF16)
    partial_back = dot_nt(gate_delta, gate_full) + dot_nt(up_delta, up_full)
    return (partial_out, partial_back, hidden, gate_delta, up_delta)


def rounded_term(left, right):
    return dot_tn(left, right).astype(BF16).astype(F32)


def slots_pass(tokens, grad_out, expert_ids, router_weight, gate_weight, up_weight, down_weight):
    devices = lax.axis_size("expert")
    token_count, model_width = tokens.shape
    per_token = expert_ids.shape[1]
    experts = router_weight.shape[1]
    halfway = token_count // 2
    capacity = 2 * token_count * per_token // devices
    slot_total = devices * capacity
    pair_count = token_count * per_token
    onehot = expert_ids[:, :, None] == jnp.arange(experts, dtype=jnp.int32)[None, None, :]
    logits = dot(tokens, router_weight)
    chosen = jnp.sum(jnp.where(onehot, logits[:, None, :], 0.0), axis=2)
    probability = jax.nn.sigmoid(chosen)
    summed = jnp.sum(probability, axis=1, keepdims=True)
    gate_share = probability / summed
    scaled = (gate_share[:, :, None] * grad_out[:, None, :].astype(F32)).astype(BF16)
    scaled = scaled.reshape(pair_count, model_width)
    named = jnp.sum(onehot.astype(BF16), axis=1).reshape(2, halfway, experts)
    order = jnp.arange(halfway, dtype=jnp.int32)
    earlier = (order[None, :] < order[:, None]).astype(BF16)
    before = jnp.einsum("st,pte->pse", earlier, named, preferred_element_type=F32)
    before = before.reshape(token_count, 1, experts)
    position = jnp.sum(jnp.where(onehot, before, 0.0), axis=2).astype(jnp.int32)
    parity = (jnp.arange(token_count, dtype=jnp.int32) // halfway)[:, None]
    target = ((2 * expert_ids + parity) * capacity + position).reshape(pair_count)
    source = (
        jnp.full((slot_total,), pair_count, jnp.int32)
        .at[target]
        .set(jnp.arange(pair_count, dtype=jnp.int32))
    )
    filled = (source < pair_count)[:, None]
    clipped = jnp.minimum(source, pair_count - 1)
    row_buffer = jnp.where(filled, jnp.take(tokens, clipped // per_token, axis=0), 0.0)
    grad_buffer = jnp.where(filled, jnp.take(scaled, clipped, axis=0), 0.0)
    row_buffer = row_buffer.reshape(devices, capacity, model_width)
    grad_buffer = grad_buffer.reshape(devices, capacity, model_width)

    def exchange(value):
        return lax.all_to_all(value, "expert", split_axis=0, concat_axis=0, tiled=True)

    rows_in = exchange(row_buffer).reshape(slot_total, model_width)
    grads_in = exchange(grad_buffer).reshape(slot_total, model_width)
    other_rows, other_grads = from_partner((rows_in, grads_in), "expert", 0)
    both_rows = jnp.concatenate([rows_in, other_rows], axis=0)
    both_grads = jnp.concatenate([grads_in, other_grads], axis=0)
    partial_out, partial_back, hidden, gate_delta, up_delta = expert_pass(
        both_rows, both_grads, gate_weight[0], up_weight[0], down_weight[0]
    )
    got_out = from_partner(partial_out[slot_total:].astype(BF16), "expert", 0).astype(F32)
    got_back = from_partner(partial_back[slot_total:].astype(BF16), "expert", 0).astype(F32)
    out_rows = (partial_out[:slot_total] + got_out).astype(BF16)
    back_rows = (partial_back[:slot_total] + got_back).astype(BF16)
    gate_sum = rounded_term(rows_in, gate_delta[:slot_total]) + rounded_term(
        other_rows, gate_delta[slot_total:]
    )
    up_sum = rounded_term(rows_in, up_delta[:slot_total]) + rounded_term(
        other_rows, up_delta[slot_total:]
    )
    down_sum = rounded_term(hidden[:slot_total], grads_in) + rounded_term(
        hidden[slot_total:], other_grads
    )
    gate_grad = gate_sum.astype(BF16)[None]
    up_grad = up_sum.astype(BF16)[None]
    down_grad = down_sum.astype(BF16)[None]
    out_back = exchange(out_rows.reshape(devices, capacity, model_width))
    grad_back = exchange(back_rows.reshape(devices, capacity, model_width))
    expert_out = jnp.take(out_back.reshape(slot_total, model_width), target, axis=0)
    expert_out = expert_out.reshape(token_count, per_token, model_width).astype(F32)
    expert_back = jnp.take(grad_back.reshape(slot_total, model_width), target, axis=0)
    expert_back = expert_back.reshape(token_count, per_token, model_width).astype(F32)
    mixed = jnp.sum(gate_share[:, :, None] * expert_out, axis=1).astype(BF16)
    gate_slope = jnp.sum(grad_out[:, None, :].astype(F32) * expert_out, axis=2)
    prob_slope = (gate_slope - jnp.sum(gate_share * gate_slope, axis=1, keepdims=True)) / summed
    logit_slope = prob_slope * probability * (1.0 - probability)
    router_delta = jnp.sum(jnp.where(onehot, logit_slope[:, :, None], 0.0), axis=1).astype(BF16)
    token_grad = jnp.sum(expert_back, axis=1) + dot_nt(router_delta, router_weight)
    token_grad = token_grad.astype(BF16)
    router_grad = lax.psum_scatter(
        dot_tn(tokens, router_delta), "expert", scatter_dimension=0, tiled=True
    )
    return (mixed, token_grad, gate_grad, up_grad, down_grad, router_grad)


def on_device(tokens, grad_out, expert_ids, router_weight, gate_weight, up_weight, down_weight):
    token_count = tokens.shape[0]
    capacity = 2 * token_count * expert_ids.shape[1] // lax.axis_size("expert")
    step = all_tokens_pass if 2 * capacity >= token_count else slots_pass
    return step(tokens, grad_out, expert_ids, router_weight, gate_weight, up_weight, down_weight)


def solution(mesh):
    return jax.shard_map(
        on_device,
        mesh=mesh,
        in_specs=(
            P(("groups", "expert"), None),
            P(("groups", "expert"), None),
            P(("groups", "expert"), None),
            P(),
            P("expert", None, None),
            P("expert", None, None),
            P("expert", None, None),
        ),
        out_specs=(
            P(("groups", "expert"), None),
            P(("groups", "expert"), None),
            P(("groups", "expert"), None, None),
            P(("groups", "expert"), None, None),
            P(("groups", "expert"), None, None),
            P(("groups", "expert"), None),
        ),
        check_vma=False,
    )
```

```python
import jax
import jax.numpy as jnp
from jax import lax
from jax.experimental import pallas as pl
from jax.experimental.pallas import tpu as pltpu
from jax.sharding import PartitionSpec as P

F32 = jnp.float32
BF16 = jnp.bfloat16


def from_partner(value, axis, distance):
    mask = 2**distance
    pairs = [(source, source ^ mask) for source in range(lax.axis_size(axis))]
    return lax.ppermute(value, axis, pairs)


def dot(left, right):
    return jnp.dot(left, right, preferred_element_type=F32)


def dot_nt(left, right):
    return lax.dot_general(left, right, (((1,), (1,)), ((), ())), preferred_element_type=F32)


def dot_tn(left, right):
    return lax.dot_general(left, right, (((0,), (0,)), ((), ())), preferred_element_type=F32)


LANES = 128
PIECES = 3
MIB = 2**20


def ring_send(value, step):
    chips = lax.axis_size("expert") // 2
    ring = list(range(0, chips, 2)) + list(range(chips - 1, 0, -2))
    pairs = [
        (2 * ring[place] + core, 2 * ring[(place + step) % chips] + core)
        for place in range(chips)
        for core in range(2)
    ]
    return lax.ppermute(value, "expert", pairs)


def after(values, *firsts):
    return lax.optimization_barrier((values, firsts))[0]


def kernel_call(body, name, outs, ins, scratch=(), flops=0, limit=8, **more):
    moved = sum(a.size * a.dtype.itemsize for a in (*ins, *outs))
    return pl.pallas_call(
        body,
        name=name,
        out_shape=outs,
        scratch_shapes=scratch,
        compiler_params=pltpu.CompilerParams(vmem_limit_bytes=limit * MIB),
        cost_estimate=pl.CostEstimate(flops=flops, bytes_accessed=moved, transcendentals=0),
        **more,
    )(*ins)


VMEM = pl.BlockSpec(memory_space=pltpu.VMEM)
ANY = pl.BlockSpec(memory_space=pl.ANY)


def in_hbm(array):
    return pltpu.with_memory_space_constraint(array, pltpu.HBM)


def lane_ids(rows):
    return lax.broadcasted_iota(jnp.int32, (rows, LANES), 1)


def pack_block(tokens, grad_out, ids):
    count, width = tokens.shape
    per_token = ids.shape[1]

    def body(tokens_ref, grads_ref, ids_hbm, block_ref, ids_ref, sems):
        copies = [
            pltpu.make_async_copy(
                ref, block_ref.at[:, pl.ds(i * width, width)], sems.at[i]
            )
            for i, ref in enumerate((tokens_ref, grads_ref))
        ]
        numbers = pltpu.make_async_copy(ids_hbm, ids_ref, sems.at[2])
        numbers.start()
        for copy in copies:
            copy.start()
        numbers.wait()
        row = lax.broadcasted_iota(jnp.int32, (per_token, LANES), 0)
        spread = (row == lane_ids(per_token)).astype(F32).astype(BF16)
        numbers = ids_ref[...].astype(F32).astype(BF16)
        block_ref[:, 2 * width :] = dot_tn(numbers, spread).astype(BF16)
        for copy in copies:
            copy.wait()

    out = jax.ShapeDtypeStruct((count, 2 * width + LANES), BF16)
    return kernel_call(
        body,
        "pack_block",
        (out,),
        (in_hbm(tokens), in_hbm(grad_out), in_hbm(ids.T)),
        scratch=[pltpu.VMEM((per_token, count), jnp.int32), pltpu.SemaphoreType.DMA((3,))],
        in_specs=[ANY] * 3,
        out_specs=[VMEM],
    )[0]


def pack_weights(own, other):
    depth, width = own[0].shape
    steps = 4
    tile = depth // steps

    def body(gate_ref, up_ref, down_ref, gate_other_ref, up_other_ref, down_other_ref, *made):
        in_ref, out_ref, in_turned_ref, out_turned_ref = made
        for i, ref in enumerate((gate_ref, gate_other_ref, up_ref, up_other_ref)):
            in_ref[:, i * width : (i + 1) * width] = ref[...]
            in_turned_ref[i * width : (i + 1) * width, :] = ref[...].T
        for i, ref in enumerate((down_ref, down_other_ref)):
            out_ref[i * width : (i + 1) * width, :] = ref[...]
            out_turned_ref[:, i * width : (i + 1) * width] = ref[...].T

    in_spec = pl.BlockSpec((tile, width), lambda d: (d, 0))
    down_spec = pl.BlockSpec((width, tile), lambda d: (0, d))
    return kernel_call(
        body,
        "pack_weights",
        (
            jax.ShapeDtypeStruct((depth, 4 * width), BF16),
            jax.ShapeDtypeStruct((2 * width, depth), BF16),
            jax.ShapeDtypeStruct((4 * width, depth), BF16),
            jax.ShapeDtypeStruct((depth, 2 * width), BF16),
        ),
        (*own, *other),
        grid=(steps,),
        in_specs=[in_spec, in_spec, down_spec] * 2,
        out_specs=[
            pl.BlockSpec((tile, 4 * width), lambda d: (d, 0)),
            pl.BlockSpec((2 * width, tile), lambda d: (0, d)),
            pl.BlockSpec((4 * width, tile), lambda d: (0, d)),
            pl.BlockSpec((tile, 2 * width), lambda d: (d, 0)),
        ],
        limit=16,
    )


def expert_chunk(blocks, weights, router, behind, where, per_token, part, wait_for=()):
    number = len(blocks)
    stride = blocks[0].shape[1]
    spans, total = [], 0
    for block in blocks:
        spans.append(slice(total, total + block.shape[0]))
        total += block.shape[0]
    width, model_width = weights[1].shape[0] // 2, weights[1].shape[1]

    def body(*refs):
        block_refs, refs = refs[:number], refs[number:]
        in_ref, down_ref, in_turned_ref, down_turned_ref = refs[:4]
        router_ref, behind_ref, where_ref = refs[4:7]
        refs = refs[7 + len(wait_for) :]
        made_refs, refs = refs[:number], refs[number:]
        hidden_refs, delta_refs = refs[:2], refs[2:4]
        side_ref, column_ref, both_ref, delta_ref = refs[4:]
        for i in range(number):
            both_ref[spans[i], :] = block_refs[i][...]
        rows = both_ref[:, :model_width]
        grads = both_ref[:, model_width : 2 * model_width]
        ids = both_ref[:, 2 * model_width :].astype(F32)
        logits = dot(rows, router_ref[...])
        named = jnp.zeros((total, LANES), F32)
        for k in range(per_token):
            named = named + jnp.where(ids[:, k : k + 1] == behind_ref[...], 1.0, 0.0)
        probability = named * jax.nn.sigmoid(logits)
        summed = jnp.sum(probability, axis=1, keepdims=True)
        gates = probability / summed
        side_ref[:, :LANES] = gates
        side_ref[:, LANES : 2 * LANES] = probability * (1.0 - probability) / summed
        gate = gates[:, :1]
        first = pl.multiple_of(where_ref[0] * 2 * part, 2 * part)
        column_ref[...] = both_ref[:, pl.ds(first, 2 * part)]
        before = dot(rows, in_ref[...])
        pre_gate, pre_up = before[:, : 2 * width], before[:, 2 * width :]
        squash = jax.nn.sigmoid(pre_gate)
        activated = pre_gate * squash
        hidden = activated * pre_up
        hidden_gated = (gate * hidden).astype(BF16)
        back_hidden = dot(grads, down_turned_ref[...])
        slope = jnp.sum(hidden * back_hidden, axis=1, keepdims=True)
        side_ref[:, 2 * LANES :] = jnp.broadcast_to(slope, (total, LANES))
        back_hidden = gate * back_hidden
        gate_delta = back_hidden * pre_up * squash * (1.0 + pre_gate * (1.0 - squash))
        gate_delta, up_delta = gate_delta.astype(BF16), (back_hidden * activated).astype(BF16)
        delta_ref[:, : 2 * width] = gate_delta
        delta_ref[:, 2 * width :] = up_delta
        for h in range(2):
            half = slice(h * width, (h + 1) * width)
            hidden_refs[h][...] = hidden_gated[:, half]
            delta_refs[h][:, :width] = gate_delta[:, half]
            delta_refs[h][:, width:] = up_delta[:, half]
        out = dot(hidden_gated, down_ref[...]).astype(BF16)
        back = dot(delta_ref[...], in_turned_ref[...]).astype(BF16)
        for i in range(number):
            made_refs[i][:, :model_width] = out[spans[i]]
            made_refs[i][:, model_width:] = back[spans[i]]

    outs = (
        *(jax.ShapeDtypeStruct((block.shape[0], 2 * model_width), BF16) for block in blocks),
        *(jax.ShapeDtypeStruct((total, width), BF16) for _ in range(2)),
        *(jax.ShapeDtypeStruct((total, 2 * width), BF16) for _ in range(2)),
        jax.ShapeDtypeStruct((total, 3 * LANES), F32),
        jax.ShapeDtypeStruct((total, 2 * part), BF16),
        jax.ShapeDtypeStruct((total, stride), BF16),
    )
    made = kernel_call(
        body,
        "expert_chunk",
        outs,
        (*blocks, *weights, router, behind, where, *wait_for),
        scratch=[pltpu.VMEM((total, 4 * width), BF16)],
        limit=20,
        flops=24 * total * model_width * width,
        in_specs=[VMEM] * (number + 6)
        + [pl.BlockSpec(memory_space=pltpu.SMEM)]
        + [ANY] * len(wait_for),
        out_specs=[VMEM] * len(outs),
    )
    return made[:number], made[number : number + 2], made[number + 2 : number + 4], made[-3:]


def first_messages(upper, lower, sides, layout):
    half, stride = upper.shape
    count = 2 * half
    chips = len(layout)

    def body(upper_ref, lower_ref, *refs):
        side_refs, (up_ref, down_ref, slopes_ref) = refs[: len(sides)], refs[len(sides) :]
        table = jnp.zeros((count, LANES), F32)
        for k, (index, offset) in enumerate(layout):
            column = side_refs[index][offset : offset + count, :]
            table = jnp.where(lane_ids(count) == k, column, table)
        packed = jnp.zeros((count, LANES), F32)
        for piece in range(PIECES):
            part = table.astype(BF16).astype(F32)
            table = table - part
            packed = packed + (part if piece == 0 else pltpu.roll(part, piece * chips, 1))
        packed = packed[:half] + pltpu.roll(packed[half:], PIECES * chips, 1)
        packed = packed.astype(BF16)
        slopes_ref[...] = packed
        up_ref[:, :stride] = upper_ref[...]
        up_ref[:, stride:] = packed
        down_ref[:, :stride] = lower_ref[...]
        down_ref[:, stride:] = packed

    outs = (
        jax.ShapeDtypeStruct((half, stride + LANES), BF16),
        jax.ShapeDtypeStruct((half, stride + LANES), BF16),
        jax.ShapeDtypeStruct((half, LANES), BF16),
    )
    slope_specs = [pl.BlockSpec((side.shape[0], LANES), lambda i: (0, 2)) for side in sides]
    return kernel_call(
        body,
        "first_messages",
        outs,
        (upper, lower, *sides),
        grid=(1,),
        in_specs=[pl.BlockSpec(upper.shape, lambda i: (0, 0))] * 2 + slope_specs,
        out_specs=[pl.BlockSpec(o.shape, lambda i: (0, 0)) for o in outs],
    )


def next_message(got, made, upper, wait_for=()):
    count, stride = made.shape
    half = count // 2
    small = got.shape[0] == half

    def body(got_ref, made_ref, *refs):
        message_ref = refs[-1]
        if small:
            near, rest = (slice(0, half), slice(half, count)) if upper else (slice(half, count), slice(0, half))
            message_ref[near, :stride] = (
                made_ref[near].astype(F32) + got_ref[:, :stride].astype(F32)
            ).astype(BF16)
            message_ref[rest, :stride] = made_ref[rest]
        else:
            message_ref[:, :stride] = (
                made_ref[...].astype(F32) + got_ref[:, :stride].astype(F32)
            ).astype(BF16)
        message_ref[:half, stride:] = got_ref[:half, stride:]
        message_ref[half:, stride:] = jnp.zeros((count - half, LANES), BF16)

    out = jax.ShapeDtypeStruct((count, stride + LANES), BF16)
    return kernel_call(
        body,
        "next_message",
        (out,),
        (got, made, *wait_for),
        flops=count * stride,
        in_specs=[VMEM] * 2 + [ANY] * len(wait_for),
        out_specs=[VMEM],
    )[0]


def weight_parts(arrived, hidden, delta, half=None, received=None, wait_for=()):
    number = len(arrived)
    total = sum(a.shape[0] for a in arrived)
    model_width = (arrived[0].shape[1] - LANES) // 2
    width = hidden[0].shape[1]
    tile = 256 if model_width % 256 == 0 else model_width
    every = model_width // tile
    steps, skip = (every, 0) if half is None else (every // 2, half * (every // 2))
    chunks = len(hidden)

    def body(*refs):
        token_refs, grad_refs = refs[:number], refs[number : 2 * number]
        hidden_refs = refs[2 * number : 2 * number + chunks]
        delta_refs = refs[2 * number + chunks : 2 * number + 2 * chunks]
        rest = refs[2 * number + 2 * chunks + len(wait_for) : -2]
        hidden_ref, delta_ref = refs[-2:]

        @pl.when(pl.program_id(0) == 0)
        def _():
            first = 0
            for i in range(chunks):
                last = first + hidden_refs[i].shape[0]
                delta_ref[first:last, :] = delta_refs[i][...]
                first = last
            hidden_ref[...] = jnp.concatenate([ref[...] for ref in hidden_refs], axis=0).T

        mark_ref = rest[-1]
        mark_ref[...] = jnp.zeros(mark_ref.shape, F32)
        rows = jnp.concatenate([ref[...] for ref in token_refs], axis=0)
        grads = jnp.concatenate([ref[...] for ref in grad_refs], axis=0)
        into = dot_tn(rows, delta_ref[...])
        down = dot(hidden_ref[...], grads)
        if received is None:
            gate_ref, up_ref, down_ref, _ = rest
            gate_ref[...] = into[:, :width].astype(BF16)
            up_ref[...] = into[:, width:].astype(BF16)
            down_ref[...] = down.astype(BF16)
        else:
            gate_ref, up_ref, down_ref, _ = rest[6:]
            early = pl.program_id(0) < every // 2
            got_gate, got_up, got_down = (
                jnp.where(early, rest[i][...], rest[3 + i][...]).astype(F32) for i in range(3)
            )
            gate_ref[0] = (into[:, :width] + got_gate).astype(BF16)
            up_ref[0] = (into[:, width:] + got_up).astype(BF16)
            down_ref[0] = (down + got_down).astype(BF16)

    def whole(a):
        return pl.BlockSpec(a.shape, lambda d: (0, 0))

    in_specs = [pl.BlockSpec((a.shape[0], tile), lambda d: (0, skip + d)) for a in arrived]
    in_specs += [pl.BlockSpec((a.shape[0], tile), lambda d: (0, every + skip + d)) for a in arrived]
    in_specs += [whole(a) for a in (*hidden, *delta)]
    in_specs += [ANY] * len(wait_for)
    ins = (*arrived, *arrived, *hidden, *delta, *wait_for)
    if received is None:
        shapes = [(model_width // 2, width)] * 2 + [(width, model_width // 2)]
        out_specs = [pl.BlockSpec((tile, width), lambda d: (d, 0))] * 2
        out_specs += [pl.BlockSpec((width, tile), lambda d: (0, d))]
    else:
        shapes = [(1, model_width, width)] * 2 + [(1, width, model_width)]
        out_specs = [pl.BlockSpec((1, tile, width), lambda d: (0, d, 0))] * 2
        out_specs += [pl.BlockSpec((1, width, tile), lambda d: (0, 0, d))]
        last = every // 2 - 1
        in_specs += [pl.BlockSpec((tile, width), lambda d: (jnp.minimum(d, last), 0))] * 2
        in_specs += [pl.BlockSpec((width, tile), lambda d: (0, jnp.minimum(d, last)))]
        in_specs += [pl.BlockSpec((tile, width), lambda d: (jnp.maximum(d - last - 1, 0), 0))] * 2
        in_specs += [pl.BlockSpec((width, tile), lambda d: (0, jnp.maximum(d - last - 1, 0)))]
        ins += received
    outs = [jax.ShapeDtypeStruct(shape, BF16) for shape in shapes]
    outs = (*outs, jax.ShapeDtypeStruct((8, LANES), F32))
    out_specs.append(pl.BlockSpec((8, LANES), lambda d: (0, 0)))
    return kernel_call(
        body,
        "weight_parts",
        outs,
        ins,
        scratch=[pltpu.VMEM((width, total), BF16), pltpu.VMEM((total, 2 * width), BF16)],
        flops=6 * total * tile * steps * width,
        grid=(steps,),
        in_specs=in_specs,
        out_specs=out_specs,
    )


def router_parts(where, pieces, passed, slopes, sides, layout, order, experts, mark):
    chips = len(layout)
    number = len(pieces)
    half, part = slopes.shape[0], pieces[0].shape[1] // 2
    count = 2 * half

    def body(where_ref, *refs):
        column_refs, refs = refs[:number], refs[number:]
        passed_refs, slopes_ref, refs = refs[: chips - 1], refs[chips - 1], refs[chips:]
        side_refs = refs[: len(sides)]
        delta_ref, keep_ref, send_ref, total_ref = refs[len(sides) + 1 :]
        tables = []
        for k in range(chips):
            packed = (slopes_ref if k == 0 else passed_refs[k - 1])[...].astype(F32)
            halves = []
            for rows in range(2):
                table = jnp.zeros((half, LANES), F32)
                for piece in range(PIECES):
                    first = (PIECES * rows + piece) * chips
                    table = table + (packed if first == 0 else pltpu.roll(packed, LANES - first, 1))
                halves.append(table)
            tables.append(jnp.concatenate(halves, axis=0))
        sub = lax.broadcasted_iota(jnp.int32, (LANES, LANES), 0)
        lane = lane_ids(LANES)
        turn = jnp.zeros((LANES, LANES), F32)
        for k in range(chips):
            turn = jnp.where((sub == k) & (lane == where_ref[2 + k]), 1.0, turn)
        turn = turn.astype(BF16)
        deltas = []
        for q in range(chips):
            slope = jnp.zeros((count, LANES), F32)
            for k in range(chips):
                from_lane = (q - k) % chips
                column = tables[k][:, from_lane : from_lane + 1]
                slope = jnp.where(lane_ids(count) == k, column, slope)
            index, offset = layout[q]
            gates = side_refs[index][offset : offset + count, :LANES]
            factor = side_refs[index][offset : offset + count, LANES : 2 * LANES]
            middle = jnp.sum(gates * slope, axis=1, keepdims=True)
            deltas.append((factor * (slope - middle)).astype(BF16))
        delta_ref[...] = deltas[0]
        deltas = [dot(delta, turn).astype(BF16) for delta in deltas]
        columns = jnp.concatenate([ref[...] for ref in column_refs], axis=0)
        total_ref[...] = dot_tn(jnp.concatenate([deltas[q] for q in order], axis=0), columns)
        core = where_ref[1]
        own, other = pl.multiple_of(core * part, part), pl.multiple_of((1 - core) * part, part)
        keep_ref[...] = total_ref[:experts, pl.ds(own, part)]
        send_ref[...] = total_ref[:experts, pl.ds(other, part)]

    in_specs = [pl.BlockSpec(a.shape, lambda i, w: (0, 0)) for a in pieces]
    in_specs += [
        pl.BlockSpec((half, LANES), lambda i, w, last=a.shape[1] // LANES - 1: (0, last))
        for a in passed
    ]
    in_specs += [pl.BlockSpec(slopes.shape, lambda i, w: (0, 0))]
    in_specs += [pl.BlockSpec((side.shape[0], 2 * LANES), lambda i, w: (0, 0)) for side in sides]
    outs = (
        jax.ShapeDtypeStruct((count, LANES), BF16),
        jax.ShapeDtypeStruct((experts, part), F32),
        jax.ShapeDtypeStruct((experts, part), F32),
    )
    in_specs += [ANY]
    ins = (where, *pieces, *passed, slopes, *sides, mark)
    return pl.pallas_call(
        body,
        name="router_parts",
        out_shape=outs,
        grid_spec=pltpu.PrefetchScalarGridSpec(
            num_scalar_prefetch=1,
            grid=(1,),
            in_specs=in_specs,
            out_specs=[pl.BlockSpec(o.shape, lambda i, w: (0, 0)) for o in outs],
            scratch_shapes=[pltpu.VMEM((LANES, 2 * part), F32)],
        ),
        compiler_params=pltpu.CompilerParams(vmem_limit_bytes=8 * MIB),
        cost_estimate=pl.CostEstimate(flops=10**7, bytes_accessed=10**6, transcendentals=0),
    )(*ins)


def last_sums(got_up, got_down, made, delta, router):
    count, stride = made.shape
    model_width = stride // 2

    def body(up_ref, down_ref, made_ref, delta_ref, router_ref, mixed_ref, grad_ref):
        total = (
            made_ref[...].astype(F32)
            + up_ref[:, :stride].astype(F32)
            + down_ref[:, :stride].astype(F32)
        )
        mixed_ref[...] = total[:, :model_width].astype(BF16)
        grad_ref[...] = (
            total[:, model_width:] + dot_nt(delta_ref[...], router_ref[...])
        ).astype(BF16)

    out = jax.ShapeDtypeStruct((count, model_width), BF16)
    return kernel_call(body, "last_sums", (out, out), (got_up, got_down, made, delta, router))


def all_tokens_pass(
    tokens, grad_out, expert_ids, router_weight, gate_weight, up_weight, down_weight
):
    chips = lax.axis_size("expert") // 2
    far = chips // 2
    count = tokens.shape[0]
    half = count // 2
    per_token = expert_ids.shape[1]
    experts = router_weight.shape[1]
    device = lax.axis_index("expert")
    chip, core = device // 2, device % 2
    place = jnp.where(chip % 2 == 0, chip // 2, chips - 1 - chip // 2)
    behind = (place - jnp.arange(chips, dtype=jnp.int32)) % chips
    behind = jnp.where(behind < far, 2 * behind, 2 * (chips - 1 - behind) + 1)
    where = jnp.concatenate([jnp.stack([chip, core]).astype(jnp.int32), behind])
    turn = (jnp.arange(experts, dtype=jnp.int32)[:, None] == behind[None, :]).astype(BF16)
    turn = jnp.pad(turn, ((0, 0), (0, LANES - chips)))
    router_turned = dot(router_weight, turn).astype(BF16)
    behind = jnp.pad(behind.astype(F32), (0, LANES - chips), constant_values=-1.0)[None]

    block = pack_block(tokens, grad_out, expert_ids)
    own = after((gate_weight[0], up_weight[0], down_weight[0]), block)
    weights = pack_weights(own, from_partner(own, "expert", 0))

    arrived = {0: block}
    made, layout, order = {}, {}, []
    hidden, delta, sides, columns, kept = ([], []), ([], []), [], [], []
    part = tokens.shape[1] // (2 * chips)

    def work(names):
        terms, hiddens, deltas, (side, column, both) = expert_chunk(
            [arrived[name] for name in names],
            weights,
            router_turned,
            behind,
            where,
            per_token,
            part,
            tuple(sides[-1:]),
        )
        offset = 0
        for name, term in zip(names, terms):
            made[name], layout[name] = term, (len(sides), offset)
            offset += term.shape[0]
        order.extend(names)
        for h in range(2):
            hidden[h].append(hiddens[h])
            delta[h].append(deltas[h])
        sides.append(side)
        columns.append(column)
        kept.append(both)

    waiting = [0]
    for k in range(1, far):
        arrived[k] = ring_send(arrived[k - 1], 1)
        arrived[chips - k] = ring_send(arrived[(chips - k + 1) % chips], -1)
        waiting += [k, chips - k]
        if k == far - 2:
            work(waiting)
            waiting = []
            for name in (k, chips - k):
                arrived[name] = after(arrived[name], *weights)
    ends = [after(arrived[name], *sides) for name in (far - 1, far + 1)]
    arrived["upper"] = ring_send(ends[0][:half], 1)
    arrived["lower"] = ring_send(ends[1][half:], -1)
    work(waiting)
    work(["upper", "lower"])
    layout[far] = layout["upper"]
    layout = [layout[k] for k in range(chips)]
    order = [far if name == "upper" else name for name in order if name != "lower"]

    up, down, slopes = first_messages(made["upper"], made["lower"], sides, layout)
    up, down = ring_send(up, 1), ring_send(down, -1)
    passed = {1: up, chips - 1: down, far: ring_send(slopes, far)}
    for distance in range(far - 1, 0, -1):
        hops = far - distance
        wait_for = ()
        if distance == 1:
            wait_for = tuple(part[-1] for part in parts)
        elif distance == far - 1:
            wait_for = (passed[far],)
        up = next_message(up, made[chips - distance], True, wait_for)
        down = next_message(down, made[distance], False, wait_for)
        before = (up, down)
        up, down = ring_send(up, 1), ring_send(down, -1)
        if distance > 1:
            passed[hops + 1], passed[chips - 1 - hops] = up, down
        if hops == 1:
            parts = [
                weight_parts(kept, hidden[1], delta[1], half=half_of, wait_for=before)
                for half_of in range(2)
            ]
            got = [from_partner(value, "expert", 0) for part_of in parts for value in part_of[:-1]]
    grads = weight_parts(kept, hidden[0], delta[0], received=tuple(got), wait_for=before)
    gate_grad, up_grad, down_grad = grads[:-1]

    router_delta, keep, send = router_parts(
        where,
        columns,
        [passed[k] for k in range(1, chips)],
        slopes,
        sides,
        layout,
        order,
        experts,
        grads[-1],
    )
    router_grad = (keep + from_partner(send, "expert", 0)).T
    mixed, token_grad = last_sums(up, down, made[0], router_delta, router_turned)
    return (mixed, token_grad, gate_grad, up_grad, down_grad, router_grad)


def expert_pass(rows, grads, gate_full, up_full, down_full):
    pre_gate = dot(rows, gate_full)
    pre_up = dot(rows, up_full)
    squash = jax.nn.sigmoid(pre_gate)
    activated = pre_gate * squash
    hidden = (activated * pre_up).astype(BF16)
    partial_out = dot(hidden, down_full)
    back_hidden = dot_nt(grads, down_full)
    gate_delta = (back_hidden * pre_up * squash * (1.0 + pre_gate * (1.0 - squash))).astype(BF16)
    up_delta = (back_hidden * activated).astype(BF16)
    partial_back = dot_nt(gate_delta, gate_full) + dot_nt(up_delta, up_full)
    return (partial_out, partial_back, hidden, gate_delta, up_delta)


def rounded_term(left, right):
    return dot_tn(left, right).astype(BF16).astype(F32)


def slots_pass(tokens, grad_out, expert_ids, router_weight, gate_weight, up_weight, down_weight):
    devices = lax.axis_size("expert")
    token_count, model_width = tokens.shape
    per_token = expert_ids.shape[1]
    experts = router_weight.shape[1]
    halfway = token_count // 2
    capacity = 2 * token_count * per_token // devices
    slot_total = devices * capacity
    pair_count = token_count * per_token
    onehot = expert_ids[:, :, None] == jnp.arange(experts, dtype=jnp.int32)[None, None, :]
    logits = dot(tokens, router_weight)
    chosen = jnp.sum(jnp.where(onehot, logits[:, None, :], 0.0), axis=2)
    probability = jax.nn.sigmoid(chosen)
    summed = jnp.sum(probability, axis=1, keepdims=True)
    gate_share = probability / summed
    scaled = (gate_share[:, :, None] * grad_out[:, None, :].astype(F32)).astype(BF16)
    scaled = scaled.reshape(pair_count, model_width)
    named = jnp.sum(onehot.astype(BF16), axis=1).reshape(2, halfway, experts)
    order = jnp.arange(halfway, dtype=jnp.int32)
    earlier = (order[None, :] < order[:, None]).astype(BF16)
    before = jnp.einsum("st,pte->pse", earlier, named, preferred_element_type=F32)
    before = before.reshape(token_count, 1, experts)
    position = jnp.sum(jnp.where(onehot, before, 0.0), axis=2).astype(jnp.int32)
    parity = (jnp.arange(token_count, dtype=jnp.int32) // halfway)[:, None]
    target = ((2 * expert_ids + parity) * capacity + position).reshape(pair_count)
    source = (
        jnp.full((slot_total,), pair_count, jnp.int32)
        .at[target]
        .set(jnp.arange(pair_count, dtype=jnp.int32))
    )
    filled = (source < pair_count)[:, None]
    clipped = jnp.minimum(source, pair_count - 1)
    row_buffer = jnp.where(filled, jnp.take(tokens, clipped // per_token, axis=0), 0.0)
    grad_buffer = jnp.where(filled, jnp.take(scaled, clipped, axis=0), 0.0)
    row_buffer = row_buffer.reshape(devices, capacity, model_width)
    grad_buffer = grad_buffer.reshape(devices, capacity, model_width)

    def exchange(value):
        return lax.all_to_all(value, "expert", split_axis=0, concat_axis=0, tiled=True)

    rows_in = exchange(row_buffer).reshape(slot_total, model_width)
    grads_in = exchange(grad_buffer).reshape(slot_total, model_width)
    other_rows, other_grads = from_partner((rows_in, grads_in), "expert", 0)
    both_rows = jnp.concatenate([rows_in, other_rows], axis=0)
    both_grads = jnp.concatenate([grads_in, other_grads], axis=0)
    partial_out, partial_back, hidden, gate_delta, up_delta = expert_pass(
        both_rows, both_grads, gate_weight[0], up_weight[0], down_weight[0]
    )
    got_out = from_partner(partial_out[slot_total:].astype(BF16), "expert", 0).astype(F32)
    got_back = from_partner(partial_back[slot_total:].astype(BF16), "expert", 0).astype(F32)
    out_rows = (partial_out[:slot_total] + got_out).astype(BF16)
    back_rows = (partial_back[:slot_total] + got_back).astype(BF16)
    gate_sum = rounded_term(rows_in, gate_delta[:slot_total]) + rounded_term(
        other_rows, gate_delta[slot_total:]
    )
    up_sum = rounded_term(rows_in, up_delta[:slot_total]) + rounded_term(
        other_rows, up_delta[slot_total:]
    )
    down_sum = rounded_term(hidden[:slot_total], grads_in) + rounded_term(
        hidden[slot_total:], other_grads
    )
    gate_grad = gate_sum.astype(BF16)[None]
    up_grad = up_sum.astype(BF16)[None]
    down_grad = down_sum.astype(BF16)[None]
    out_back = exchange(out_rows.reshape(devices, capacity, model_width))
    grad_back = exchange(back_rows.reshape(devices, capacity, model_width))
    expert_out = jnp.take(out_back.reshape(slot_total, model_width), target, axis=0)
    expert_out = expert_out.reshape(token_count, per_token, model_width).astype(F32)
    expert_back = jnp.take(grad_back.reshape(slot_total, model_width), target, axis=0)
    expert_back = expert_back.reshape(token_count, per_token, model_width).astype(F32)
    mixed = jnp.sum(gate_share[:, :, None] * expert_out, axis=1).astype(BF16)
    gate_slope = jnp.sum(grad_out[:, None, :].astype(F32) * expert_out, axis=2)
    prob_slope = (gate_slope - jnp.sum(gate_share * gate_slope, axis=1, keepdims=True)) / summed
    logit_slope = prob_slope * probability * (1.0 - probability)
    router_delta = jnp.sum(jnp.where(onehot, logit_slope[:, :, None], 0.0), axis=1).astype(BF16)
    token_grad = jnp.sum(expert_back, axis=1) + dot_nt(router_delta, router_weight)
    token_grad = token_grad.astype(BF16)
    router_grad = lax.psum_scatter(
        dot_tn(tokens, router_delta), "expert", scatter_dimension=0, tiled=True
    )
    return (mixed, token_grad, gate_grad, up_grad, down_grad, router_grad)


def on_device(tokens, grad_out, expert_ids, router_weight, gate_weight, up_weight, down_weight):
    token_count = tokens.shape[0]
    capacity = 2 * token_count * expert_ids.shape[1] // lax.axis_size("expert")
    step = all_tokens_pass if 2 * capacity >= token_count else slots_pass
    return step(tokens, grad_out, expert_ids, router_weight, gate_weight, up_weight, down_weight)


def solution(mesh):
    return jax.shard_map(
        on_device,
        mesh=mesh,
        in_specs=(
            P(("groups", "expert"), None),
            P(("groups", "expert"), None),
            P(("groups", "expert"), None),
            P(),
            P("expert", None, None),
            P("expert", None, None),
            P("expert", None, None),
        ),
        out_specs=(
            P(("groups", "expert"), None),
            P(("groups", "expert"), None),
            P(("groups", "expert"), None, None),
            P(("groups", "expert"), None, None),
            P(("groups", "expert"), None, None),
            P(("groups", "expert"), None),
        ),
        check_vma=False,
    )
```
